256 devices in a mesh: space: 64 (over y, x, z_hi), member: 4 (over z_lo, core).
Axes of the slice: x: 4, y: 4, z: 8 (z_hi: 4, z_lo: 2; z = z_hi * 2 + z_lo), core: 2. Of those that a mesh axis runs over, the one named last changes fastest.
Arguments:
- positions: float32 [1024, 3, 128], P('space'), may hold values from -6 to 6
- features: bfloat16 [1024, 128, 128], P('space'), may hold values from -6 to 6
- nbr_list: int32 [1024, 6], P('space'), may hold values from 0 to 1023, as said below
- nbr_count: int32 [1024], P('space'), may hold values from 3 to 6, as said below
- w_embed: bfloat16 [4, 128, 128], P('member'), may hold values from -0.5 to 0.5
- w_proj: bfloat16 [4, 128, 512], P('member'), may hold values from -0.5 to 0.5
- rates: float32 [4, 4], P('member'), may hold values from 0.05 to 1
Outputs:
- mean_force: float32 [1024, 3, 128], P('space')
- variance_grad: float32 [1024, 3, 128], P('space')
The draws below stay inside these ranges and needn't reach their ends.
Inputs may be any that keep to these rules, and one draw needn't show every extreme that they name: `nbr_list`: with q = b // 16 the domain of block b, taken cyclically over the 64 domains: slot 0 names b itself, slot 1 a block of domain q - 1, slot 2 a block of domain q + 1, every other slot a block of domain q - 1, q or q + 1. `nbr_count`: block 0 has all 6 slots live and block 1 exactly 3.
All inputs are finite; a program needn't handle non-finite values.
Results may differ from the reference program's by a relative error of at most 0.0017.
Values may be sent and summed in bfloat16 or wider, within the bound.
No kernel may reach another device: no remote copies, remote signals or barrier semaphores. Data moves between devices by JAX's collectives and lax.ppermute only.
A program may use at most 128 MiB of HBM per device.

```python
import math
import jax
import jax.numpy as jnp
from jax import lax

C = 128
K = 4
BLK = 128
NBR = 6
OWN = 16
NBLOCKS = 1024
MEMBERS = 4


def draw_nbr_list(key, part):
    domains = NBLOCKS // OWN
    key_offset, key_pick = jax.random.split(jax.random.fold_in(key, 11))
    offsets = jax.random.randint(key_offset, (NBLOCKS, NBR), -1, 2)
    offsets = offsets.at[:, 0].set(0)
    offsets = offsets.at[:, 1].set(-1)
    offsets = offsets.at[:, 2].set(1)
    picks = jax.random.randint(key_pick, (NBLOCKS, NBR), 0, OWN)
    block_ids = jnp.arange(NBLOCKS)[:, None]
    owners = block_ids // OWN
    neighbour_ids = jnp.mod(owners + offsets, domains) * OWN + picks
    neighbour_ids = neighbour_ids.at[:, 0].set(block_ids[:, 0])
    return neighbour_ids.astype(jnp.int32)


def draw_nbr_count(key, part):
    counts = jax.random.randint(jax.random.fold_in(key, 23), (NBLOCKS,), 3, NBR + 1)
    counts = counts.at[0].set(NBR)
    counts = counts.at[1].set(3)
    return counts.astype(jnp.int32)


def levels(key, shape, cuts, low, top_value):
    def one(position, parts):
        draws = jax.random.uniform(jax.random.fold_in(jax.random.fold_in(key, 6), position), (parts,), jnp.float32, low / len(cuts), top_value / len(cuts))
        return jnp.repeat(jnp.exp(draws), shape[position] // parts).reshape((-1,) + (1,) * (len(shape) - position - 1))

    gain = one(*cuts[0])
    for cut in cuts[1:]:
        gain = gain * one(*cut)
    return gain


def gaussian(own_key, shape, deviation, most, pieces=(), dtype=jnp.bfloat16):
    level = levels(own_key, shape, pieces, -0.22, 0.18) if pieces else 1.0
    array = jax.random.normal(own_key, shape, jnp.float32) * deviation * level
    return jnp.minimum(jnp.maximum(array, -most), most).astype(dtype)


def setup_inputs(seed: int = 0) -> dict:
    keys = jax.random.split(jax.random.key(seed), 8)
    positions = gaussian(keys[0], (NBLOCKS, 3, BLK), 1.0, 6.0, ((0, 64),), jnp.float32)
    features = gaussian(keys[1], (NBLOCKS, BLK, C), 1.0, 6.0, ((0, 64),))
    nbr_list = draw_nbr_list(jax.random.fold_in(keys[7], 71), 0)
    nbr_count = draw_nbr_count(jax.random.fold_in(keys[7], 71), 0)
    w_embed = gaussian(keys[4], (MEMBERS, C, C), C ** -0.5, 0.5, ((0, 4),))
    w_proj = gaussian(keys[5], (MEMBERS, C, K * C), C ** -0.5, 0.5, ((0, 4),))
    rates = jnp.clip(jnp.exp(math.log(1.0) - 2.9957323 * jax.random.uniform(keys[6], (MEMBERS, K), jnp.float32) ** levels(keys[6], (MEMBERS, K), ((0, 4),), -0.2, 0.2)), 0.05, 1.0)
    return dict(positions=positions, features=features, nbr_list=nbr_list, nbr_count=nbr_count, w_embed=w_embed, w_proj=w_proj, rates=rates)


def pair_terms(left_proj, right_proj, left_pos, right_pos, rate_row, channels, escale):
    contraction = jnp.einsum('ikc,jkc->kij', left_proj.astype(jnp.float32), right_proj.astype(jnp.float32)) / math.sqrt(channels)
    separation = left_pos[:, :, None] - right_pos[:, None, :]
    square = lax.optimization_barrier(jnp.sum(separation * separation, axis=0))
    radial = jnp.exp(-rate_row[:, None, None] * square[None])
    weighted = radial * contraction
    latent = lax.optimization_barrier(jnp.sum(weighted, axis=0))
    latent_slope = -lax.optimization_barrier(jnp.sum(rate_row[:, None, None] * weighted, axis=0))
    latent_bend = lax.optimization_barrier(jnp.sum((rate_row * rate_row)[:, None, None] * weighted, axis=0))
    gate_value = jax.nn.sigmoid(latent)
    first_deriv = gate_value * (1.0 + latent * (1.0 - gate_value))
    second_deriv = gate_value * (1.0 - gate_value) * (2.0 + latent * (1.0 - 2.0 * gate_value))
    first_term = escale * first_deriv * latent_slope
    second_term = escale * (second_deriv * latent_slope * latent_slope + first_deriv * latent_bend)
    return (separation, first_term, second_term)

def reference(positions, features, nbr_list, nbr_count, w_embed, w_proj, rates):
    escale = 1.0 / math.sqrt(NBR * BLK)
    in_use = (jnp.arange(NBR)[None, :] < nbr_count[:, None]).astype(jnp.float32)
    block_ids = jnp.arange(NBLOCKS)
    member_forces = []
    member_projs = []
    for member in range(MEMBERS):
        hidden = jax.nn.silu(jnp.dot(features.reshape(NBLOCKS * BLK, C), w_embed[member], preferred_element_type=jnp.float32)).astype(jnp.bfloat16)
        projected = jnp.dot(hidden, w_proj[member], preferred_element_type=jnp.float32).astype(jnp.bfloat16).reshape(NBLOCKS, BLK, K, C)
        rate_row = rates[member]

        def block_terms(block_index, projected=projected, rate_row=rate_row):
            neighbours = nbr_list[block_index]

            def one_slot(right_proj, right_pos):
                return pair_terms(projected[block_index], right_proj, positions[block_index], right_pos, rate_row, C, escale)
            separation, first_term, second_term = jax.vmap(one_slot)(projected[neighbours], positions[neighbours])
            slot_mask = in_use[block_index][:, None, None]
            return (separation, first_term * slot_mask, second_term * slot_mask)

        def force_block(block_index, block_terms=block_terms):
            separation, first_term, second_term = block_terms(block_index)
            return -2.0 * lax.optimization_barrier(jnp.sum(first_term[:, None] * separation, axis=(0, 3)))
        member_forces.append(lax.map(force_block, block_ids))
        member_projs.append(block_terms)
    force_total = member_forces[0]
    for member in range(1, MEMBERS):
        force_total = force_total + member_forces[member]
    mean_force = force_total / MEMBERS
    variance_grad = jnp.zeros((NBLOCKS, 3, BLK), jnp.float32)
    for member in range(MEMBERS):
        tangent = 2.0 / MEMBERS * (member_forces[member] - mean_force)
        block_terms = member_projs[member]

        def grad_block(block_index, tangent=tangent, block_terms=block_terms):
            separation, first_term, second_term = block_terms(block_index)
            left_tangent = tangent[block_index]
            right_tangent = tangent[nbr_list[block_index]]
            change = right_tangent[:, :, None, :] - left_tangent[None, :, :, None]
            radial_dot = lax.optimization_barrier(jnp.sum(separation * change, axis=1))
            hessian_vec = 2.0 * first_term[:, None] * change + 4.0 * (second_term * radial_dot)[:, None] * separation
            return lax.optimization_barrier(jnp.sum(hessian_vec, axis=(0, 3)))
        variance_grad = variance_grad + lax.map(grad_block, block_ids)
    return (mean_force, variance_grad)
```

```python
import math

import jax
import jax.numpy as jnp
from jax import lax
from jax.experimental import pallas as pl
from jax.experimental.pallas import tpu as pltpu
from jax.sharding import PartitionSpec as P

STEP_BLOCKS = 4
CHUNK = 32
LOG2E = 1.4426950408889634


def ring(axis, shift):
    count = lax.axis_size(axis)
    return [(i, (i + shift) % count) for i in range(count)]


def flip(axis, bit):
    return [(i, i ^ bit) for i in range(lax.axis_size(axis))]


def columns(tile):
    rows = jnp.concatenate([tile, jnp.zeros((8 - tile.shape[0], tile.shape[1]), jnp.float32)], axis=0)
    return jnp.transpose(rows)


def pair_kernel(
    idx_ref, cnt_ref, rate_ref, core_ref,
    own_ref, lo_a, lo_b, hi_a, hi_b, embed_ref, wproj_ref,
    pos_own, pos_lo, pos_hi,
    force_ref, first_ref, second_ref,
    proj_ref, col_ref,
):
    owned = own_ref.shape[0]
    half = lo_a.shape[0]
    slots = first_ref.shape[1]
    rows = first_ref.shape[2]
    channels = own_ref.shape[2]
    bases = wproj_ref.shape[1] // channels
    escale = 1.0 / math.sqrt(slots * rows)
    sigma = 1.0 / math.sqrt(channels)
    step = pl.program_id(0)

    @pl.when(step == 0)
    def _():
        def project(source, base):
            def one(i, carry):
                x = source[pl.ds(2 * i, 2)].reshape(2 * rows, channels)
                h = jnp.dot(x, embed_ref[...], preferred_element_type=jnp.float32)
                half_h = 0.5 * h
                hidden = (half_h + half_h * jnp.tanh(half_h)).astype(jnp.bfloat16)
                out = jnp.dot(hidden, wproj_ref[...], preferred_element_type=jnp.float32)
                proj_ref[pl.ds(base + 2 * i, 2)] = out.astype(jnp.bfloat16).reshape(2, rows, bases * channels)
                return carry

            lax.fori_loop(0, source.shape[0] // 2, one, 0, unroll=2)

        core = core_ref[0]
        near = core * half
        far = half - near
        project(own_ref, owned)
        project(lo_a, near)
        project(lo_b, far)
        project(hi_a, 2 * owned + near)
        project(hi_b, 2 * owned + far)

        def spread(source, base):
            def one(i, carry):
                col_ref[base + i] = columns(source[i])
                return carry

            lax.fori_loop(0, owned, one, 0, unroll=4)

        spread(pos_lo, 0)
        spread(pos_own, owned)
        spread(pos_hi, 2 * owned)

    decay = [-LOG2E * rate_ref[k] for k in range(bases)]
    slope_coef = [(-2.0 * sigma) * rate_ref[k] for k in range(bases)]
    bend_coef = [(4.0 * sigma) * rate_ref[k] * rate_ref[k] for k in range(bases)]

    for part in range(STEP_BLOCKS):
        block = step * STEP_BLOCKS + part
        count = cnt_ref[block]

        def run(live, block=block, part=part):
            left = proj_ref[owned + block]
            left_pos = [pos_own[block, pl.ds(a, 1), :] for a in range(3)]
            total = [jnp.zeros((8, rows), jnp.float32) for _ in range(3)]
            for slot in range(live):
                source = idx_ref[block * slots + slot]
                dots = [
                    lax.dot_general(
                        proj_ref[source, :, k * channels:(k + 1) * channels],
                        left[:, k * channels:(k + 1) * channels],
                        (((1,), (1,)), ((), ())),
                        preferred_element_type=jnp.float32,
                    )
                    for k in range(bases)
                ]
                for start in range(0, rows, CHUNK):
                    cols = col_ref[source, start:start + CHUNK, :]
                    delta = [left_pos[a] - cols[:, a:a + 1] for a in range(3)]
                    square = delta[0] * delta[0] + delta[1] * delta[1] + delta[2] * delta[2]
                    w = [
                        jnp.exp2(decay[k] * square) * dots[k][start:start + CHUNK]
                        for k in range(bases)
                    ]
                    lh = (0.5 * sigma) * sum(w[1:], w[0])
                    slope = sum([slope_coef[k] * w[k] for k in range(1, bases)], slope_coef[0] * w[0])
                    bend = sum([bend_coef[k] * w[k] for k in range(1, bases)], bend_coef[0] * w[0])
                    h = jnp.tanh(lh)
                    u = 1.0 - h * h
                    p1 = (1.0 + h) + lh * u
                    p2 = u * (1.0 - lh * h)
                    first = p1 * slope
                    second = p2 * (slope * slope) + p1 * bend
                    first_ref[part, slot, start:start + CHUNK, :] = first
                    second_ref[part, slot, start:start + CHUNK, :] = second
                    for a in range(3):
                        total[a] = total[a] + jnp.sum((first * delta[a]).reshape(CHUNK // 8, 8, rows), axis=0)
            force_ref[part] = jnp.concatenate(
                [(-0.5 * escale) * jnp.sum(t, axis=0, keepdims=True) for t in total], axis=0
            )

        for live in range(3, slots + 1):
            pl.when(count == live)(lambda live=live: run(live))


def grad_kernel(
    idx_ref, cnt_ref, pos_own, pos_lo, pos_hi, tan_own, tan_lo, tan_hi, first_ref, second_ref,
    grad_ref, col_ref,
):
    owned = pos_own.shape[0]
    slots = first_ref.shape[1]
    rows = first_ref.shape[2]
    escale = 1.0 / math.sqrt(slots * rows)
    step = pl.program_id(0)

    @pl.when(step == 0)
    def _():
        def spread(pos, tan, base):
            def one(i, carry):
                col_ref[base + i] = columns(jnp.concatenate([pos[i], tan[i]], axis=0))
                return carry

            lax.fori_loop(0, owned, one, 0, unroll=4)

        spread(pos_lo, tan_lo, 0)
        spread(pos_own, tan_own, owned)
        spread(pos_hi, tan_hi, 2 * owned)

    for part in range(STEP_BLOCKS):
        block = step * STEP_BLOCKS + part
        count = cnt_ref[block]

        def run(live, block=block, part=part):
            left_pos = [pos_own[block, pl.ds(a, 1), :] for a in range(3)]
            left_tan = [tan_own[block, pl.ds(a, 1), :] for a in range(3)]
            total = [jnp.zeros((8, rows), jnp.float32) for _ in range(3)]
            for slot in range(live):
                source = idx_ref[block * slots + slot]
                for start in range(0, rows, CHUNK):
                    cols = col_ref[source, start:start + CHUNK, :]
                    delta = [left_pos[a] - cols[:, a:a + 1] for a in range(3)]
                    change = [cols[:, 3 + a:4 + a] - left_tan[a] for a in range(3)]
                    first = first_ref[part, slot, start:start + CHUNK, :]
                    second = second_ref[part, slot, start:start + CHUNK, :]
                    along = second * (delta[0] * change[0] + delta[1] * change[1] + delta[2] * change[2])
                    for a in range(3):
                        term = first * change[a] + along * delta[a]
                        total[a] = total[a] + jnp.sum(term.reshape(CHUNK // 8, 8, rows), axis=0)
            grad_ref[part] = jnp.concatenate(
                [(0.5 * escale) * jnp.sum(t, axis=0, keepdims=True) for t in total], axis=0
            )

        for live in range(3, slots + 1):
            pl.when(count == live)(lambda live=live: run(live))


def whole(array):
    return pl.BlockSpec(array.shape, lambda *_: (0,) * array.ndim, pipeline_mode=pl.Buffered(1))


def stepped(shape):
    return pl.BlockSpec((STEP_BLOCKS,) + shape, lambda i, *_: (i,) + (0,) * len(shape))


def member_sum(array):
    size = lax.axis_size("member")
    others = [lax.ppermute(array, "member", flip("member", bit)) for bit in range(1, size)]
    return array + others[0] + (others[1] + others[2])


def body(positions, features, nbr_list, nbr_count, w_embed, w_proj, rates):
    owned, dims, rows = positions.shape
    channels = features.shape[2]
    slots = nbr_list.shape[1]
    width = w_proj.shape[2]
    domains = lax.axis_size("space")
    members = lax.axis_size("member")
    domain = lax.axis_index("space")
    core = lax.axis_index("member") % 2
    up, down = ring("space", 1), ring("space", -1)
    half = owned // 2

    mine = lax.dynamic_slice_in_dim(features, core * half, half, 0)
    lo_a = lax.ppermute(mine, "space", up)
    hi_a = lax.ppermute(mine, "space", down)
    pos_lo = lax.ppermute(positions, "space", up)
    pos_hi = lax.ppermute(positions, "space", down)
    swap = flip("member", 1)
    lo_b = lax.ppermute(lo_a, "member", swap)
    hi_b = lax.ppermute(hi_a, "member", swap)

    index = jnp.mod(nbr_list - (domain - 1) * owned, domains * owned).reshape(-1)
    core_arr = core.astype(jnp.int32).reshape(1)
    pairs = jax.ShapeDtypeStruct((owned, slots, rows, rows), jnp.float32)
    small = jax.ShapeDtypeStruct((owned, dims, rows), jnp.float32)
    tensors = (features, lo_a, lo_b, hi_a, hi_b, w_embed[0], w_proj[0], positions, pos_lo, pos_hi)
    force, first, second = pl.pallas_call(
        pair_kernel,
        grid_spec=pltpu.PrefetchScalarGridSpec(
            num_scalar_prefetch=4,
            grid=(owned // STEP_BLOCKS,),
            in_specs=[whole(t) for t in tensors],
            out_specs=[stepped((dims, rows)), stepped((slots, rows, rows)), stepped((slots, rows, rows))],
            scratch_shapes=[
                pltpu.VMEM((3 * owned, rows, width), jnp.bfloat16),
                pltpu.VMEM((3 * owned, rows, 8), jnp.float32),
            ],
        ),
        out_shape=[small, pairs, pairs],
        name="pair_forces",
    )(index, nbr_count, rates[0], core_arr, *tensors)

    mean_force = member_sum(force) / members
    tangent = (2.0 / members) * (force - mean_force)
    tan_lo = lax.ppermute(tangent, "space", up)
    tan_hi = lax.ppermute(tangent, "space", down)
    tensors = (positions, pos_lo, pos_hi, tangent, tan_lo, tan_hi)
    grad = pl.pallas_call(
        grad_kernel,
        grid_spec=pltpu.PrefetchScalarGridSpec(
            num_scalar_prefetch=2,
            grid=(owned // STEP_BLOCKS,),
            in_specs=[whole(t) for t in tensors] + [stepped((slots, rows, rows))] * 2,
            out_specs=stepped((dims, rows)),
            scratch_shapes=[pltpu.VMEM((3 * owned, rows, 8), jnp.float32)],
        ),
        out_shape=small,
        name="variance_gradient",
    )(index, nbr_count, *tensors, first, second)
    return (mean_force, member_sum(grad))


def solution(mesh):
    return jax.shard_map(
        body,
        mesh=mesh,
        in_specs=(
            P("space", None, None),
            P("space", None, None),
            P("space", None),
            P("space"),
            P("member", None, None),
            P("member", None, None),
            P("member", None),
        ),
        out_specs=(P("space", None, None), P("space", None, None)),
        check_vma=False,
    )
```

```python
import math

import jax
import jax.numpy as jnp
from jax import lax
from jax.experimental import pallas as pl
from jax.experimental.pallas import tpu as pltpu
from jax.sharding import PartitionSpec as P

STEP_BLOCKS = 4
CHUNK = 32
PIECES = 3
TILE = 16
LOG2E = 1.4426950408889634


def ring(axis, shift):
    count = lax.axis_size(axis)
    return [(i, (i + shift) % count) for i in range(count)]


def flip(axis, bit):
    return [(i, i ^ bit) for i in range(lax.axis_size(axis))]


def place(rows, row, value):
    at = lax.broadcasted_iota(jnp.int32, rows.shape, 0) == row
    return jnp.where(at, value, rows)


def pattern(depth, base, axis, width, value):
    row = lax.broadcasted_iota(jnp.int32, (depth, width), 0)
    hit = row == base + axis
    for piece in range(1, PIECES):
        hit = hit | (row == base + 3 * piece + axis)
    return jnp.where(hit, value, 0.0)


def difference_rhs(rows, axis, depth):
    rhs = pattern(depth, 0, axis, rows.shape[1], -1.0)
    for piece in range(PIECES):
        at = 3 * piece + axis
        rhs = place(rhs, 3 * PIECES + piece, rows[at:at + 1])
    return rhs.astype(jnp.bfloat16)


def change_rhs(pieces, axis, depth):
    rhs = pattern(depth, TILE, axis, pieces[0].shape[1], 1.0)
    for piece in range(PIECES):
        rhs = place(rhs, 3 * PIECES + piece, -pieces[piece][axis:axis + 1])
    return rhs.astype(jnp.bfloat16)


def split(array):
    pieces = []
    rest = array
    for _ in range(PIECES):
        piece = rest.astype(jnp.bfloat16).astype(jnp.float32)
        pieces.append(piece)
        rest = rest - piece
    return pieces


def pair_kernel(
    idx_ref, cnt_ref, rate_ref, core_ref,
    own_ref, lo_a, lo_b, hi_a, hi_b, embed_ref, wproj_ref,
    force_ref, first_ref, second_ref, rows_ref,
    proj_ref, col_ref,
):
    owned = own_ref.shape[0]
    half = lo_a.shape[0]
    slots = first_ref.shape[1]
    rows = first_ref.shape[2]
    channels = own_ref.shape[2]
    bases = wproj_ref.shape[1] // channels
    escale = 1.0 / math.sqrt(slots * rows)
    sigma = 1.0 / math.sqrt(channels)
    step = pl.program_id(0)

    @pl.when(step == 0)
    def _():
        def project(source, base):
            def one(i, carry):
                x = source[pl.ds(2 * i, 2), pl.ds(0, rows), :].reshape(2 * rows, channels)
                h = jnp.dot(x, embed_ref[...], preferred_element_type=jnp.float32)
                half_h = 0.5 * h
                hidden = (half_h + half_h * jnp.tanh(half_h)).astype(jnp.bfloat16)
                out = jnp.dot(hidden, wproj_ref[...], preferred_element_type=jnp.float32)
                proj_ref[pl.ds(base + 2 * i, 2)] = out.astype(jnp.bfloat16).reshape(2, rows, bases * channels)
                for j in range(2):
                    tile = source[2 * i + j, pl.ds(rows, TILE), :]
                    rows_ref[base + 2 * i + j] = tile
                    col_ref[base + 2 * i + j] = jnp.transpose(tile.astype(jnp.float32)).astype(jnp.bfloat16)
                return carry

            lax.fori_loop(0, source.shape[0] // 2, one, 0, unroll=2)

        near = core_ref[0] * half
        far = half - near
        project(own_ref, owned)
        project(lo_a, near)
        project(lo_b, far)
        project(hi_a, 2 * owned + near)
        project(hi_b, 2 * owned + far)

    decay = [-LOG2E * rate_ref[k] for k in range(bases)]
    slope_coef = [(-2.0 * sigma) * rate_ref[k] for k in range(bases)]
    bend_coef = [(4.0 * sigma) * rate_ref[k] * rate_ref[k] for k in range(bases)]

    def one_block(part, carry):
        block = step * STEP_BLOCKS + part
        count = cnt_ref[block]

        def run(live):
            left = proj_ref[owned + block]
            tile = own_ref[block, pl.ds(rows, TILE), :].astype(jnp.float32)
            separators = [difference_rhs(tile, a, TILE) for a in range(3)]
            total = [jnp.zeros((8, rows), jnp.float32) for _ in range(3)]
            for slot in range(live):
                source = idx_ref[block * slots + slot]
                cols = col_ref[source]
                parts = [jnp.dot(cols, r, preferred_element_type=jnp.float32) for r in separators]
                dots = [
                    lax.dot_general(
                        proj_ref[source, :, k * channels:(k + 1) * channels],
                        left[:, k * channels:(k + 1) * channels],
                        (((1,), (1,)), ((), ())),
                        preferred_element_type=jnp.float32,
                    )
                    for k in range(bases)
                ]
                for start in range(0, rows, CHUNK):
                    delta = [p[start:start + CHUNK] for p in parts]
                    square = delta[0] * delta[0] + delta[1] * delta[1] + delta[2] * delta[2]
                    w = [
                        jnp.exp2(decay[k] * square) * dots[k][start:start + CHUNK]
                        for k in range(bases)
                    ]
                    lh = (0.5 * sigma) * sum(w[1:], w[0])
                    slope = sum([slope_coef[k] * w[k] for k in range(1, bases)], slope_coef[0] * w[0])
                    bend = sum([bend_coef[k] * w[k] for k in range(1, bases)], bend_coef[0] * w[0])
                    h = jnp.tanh(lh)
                    u = 1.0 - h * h
                    p1 = (1.0 + h) + lh * u
                    p2 = u * (1.0 - lh * h)
                    first = p1 * slope
                    second = p2 * (slope * slope) + p1 * bend
                    first_ref[part, slot, start:start + CHUNK, :] = first
                    second_ref[part, slot, start:start + CHUNK, :] = second
                    for a in range(3):
                        total[a] = total[a] + jnp.sum((first * delta[a]).reshape(CHUNK // 8, 8, rows), axis=0)
            force_ref[part] = jnp.concatenate(
                [(-0.5 * escale) * jnp.sum(t, axis=0, keepdims=True) for t in total], axis=0
            )

        for live in range(3, slots + 1):
            pl.when(count == live)(lambda live=live: run(live))
        return carry

    lax.fori_loop(0, STEP_BLOCKS, one_block, 0)


def grad_kernel(
    idx_ref, cnt_ref, pos_ref, tan_own, tan_lo, tan_hi, first_ref, second_ref,
    grad_ref, col_ref,
):
    owned = tan_own.shape[0]
    slots = first_ref.shape[1]
    rows = first_ref.shape[2]
    escale = 1.0 / math.sqrt(slots * rows)
    step = pl.program_id(0)

    @pl.when(step == 0)
    def _():
        def spread(tan, base):
            def one(i, carry):
                filler = jnp.zeros((TILE - 3 * PIECES, rows), jnp.float32)
                tile = jnp.concatenate(
                    [pos_ref[base + i].astype(jnp.float32)] + split(tan[i]) + [filler], axis=0
                )
                col_ref[base + i] = jnp.transpose(tile).astype(jnp.bfloat16)
                return carry

            lax.fori_loop(0, owned, one, 0, unroll=4)

        spread(tan_lo, 0)
        spread(tan_own, owned)
        spread(tan_hi, 2 * owned)

    def one_block(part, carry):
        block = step * STEP_BLOCKS + part
        count = cnt_ref[block]

        def run(live):
            tile = pos_ref[owned + block].astype(jnp.float32)
            pieces = split(tan_own[block])
            sides = [difference_rhs(tile, a, 2 * TILE) for a in range(3)]
            sides += [change_rhs(pieces, a, 2 * TILE) for a in range(3)]
            total = [jnp.zeros((8, rows), jnp.float32) for _ in range(3)]
            for slot in range(live):
                source = idx_ref[block * slots + slot]
                cols = col_ref[source]
                parts = [jnp.dot(cols, r, preferred_element_type=jnp.float32) for r in sides]
                for start in range(0, rows, CHUNK):
                    delta = [p[start:start + CHUNK] for p in parts[:3]]
                    change = [p[start:start + CHUNK] for p in parts[3:]]
                    first = first_ref[part, slot, start:start + CHUNK, :]
                    second = second_ref[part, slot, start:start + CHUNK, :]
                    along = second * (delta[0] * change[0] + delta[1] * change[1] + delta[2] * change[2])
                    for a in range(3):
                        term = first * change[a] + along * delta[a]
                        total[a] = total[a] + jnp.sum(term.reshape(CHUNK // 8, 8, rows), axis=0)
            grad_ref[part] = jnp.concatenate(
                [(0.5 * escale) * jnp.sum(t, axis=0, keepdims=True) for t in total], axis=0
            )

        for live in range(3, slots + 1):
            pl.when(count == live)(lambda live=live: run(live))
        return carry

    lax.fori_loop(0, STEP_BLOCKS, one_block, 0)


def pack(features, positions):
    blocks, dims, rows = positions.shape
    pieces = []
    rest = positions
    for _ in range(PIECES):
        piece = lax.reduce_precision(rest, 8, 7)
        pieces.append(piece.astype(jnp.bfloat16))
        rest = rest - piece
    ones = jnp.ones((blocks, PIECES, rows), jnp.bfloat16)
    zeros = jnp.zeros((blocks, TILE - PIECES * (dims + 1), rows), jnp.bfloat16)
    return jnp.concatenate([features] + pieces + [ones, zeros], axis=1)


def whole(array):
    return pl.BlockSpec(array.shape, lambda *_: (0,) * len(array.shape), pipeline_mode=pl.Buffered(1))


def stepped(shape):
    return pl.BlockSpec((STEP_BLOCKS,) + shape, lambda i, *_: (i,) + (0,) * len(shape))


def member_sum(array):
    size = lax.axis_size("member")
    others = [lax.ppermute(array, "member", flip("member", bit)) for bit in range(1, size)]
    return array + others[0] + (others[1] + others[2])


def body(positions, features, nbr_list, nbr_count, w_embed, w_proj, rates):
    owned, dims, rows = positions.shape
    channels = features.shape[2]
    slots = nbr_list.shape[1]
    width = w_proj.shape[2]
    domains = lax.axis_size("space")
    members = lax.axis_size("member")
    domain = lax.axis_index("space")
    core = lax.axis_index("member") % 2
    up, down = ring("space", 1), ring("space", -1)
    half = owned // 2

    packed = pack(features, positions)
    mine = lax.dynamic_slice_in_dim(packed, core * half, half, 0)
    lo_a = lax.ppermute(mine, "space", up)
    hi_a = lax.ppermute(mine, "space", down)
    swap = flip("member", 1)
    lo_b = lax.ppermute(lo_a, "member", swap)
    hi_b = lax.ppermute(hi_a, "member", swap)

    index = jnp.mod(nbr_list - (domain - 1) * owned, domains * owned).reshape(-1)
    core_arr = core.astype(jnp.int32).reshape(1)
    pairs = jax.ShapeDtypeStruct((owned, slots, rows, rows), jnp.float32)
    small = jax.ShapeDtypeStruct((owned, dims, rows), jnp.float32)
    tensors = (packed, lo_a, lo_b, hi_a, hi_b, w_embed[0], w_proj[0])
    tiles = jax.ShapeDtypeStruct((3 * owned, TILE, rows), jnp.bfloat16)
    force, first, second, pos_rows = pl.pallas_call(
        pair_kernel,
        grid_spec=pltpu.PrefetchScalarGridSpec(
            num_scalar_prefetch=4,
            grid=(owned // STEP_BLOCKS,),
            in_specs=[whole(t) for t in tensors],
            out_specs=[stepped((dims, rows)), stepped((slots, rows, rows)), stepped((slots, rows, rows)), whole(tiles)],
            scratch_shapes=[
                pltpu.VMEM((3 * owned, rows, width), jnp.bfloat16),
                pltpu.VMEM((3 * owned, rows, TILE), jnp.bfloat16),
            ],
        ),
        out_shape=[small, pairs, pairs, tiles],
        name="pair_forces",
    )(index, nbr_count, rates[0], core_arr, *tensors)

    mean_force = member_sum(force) / members
    tangent = (2.0 / members) * (force - mean_force)
    tan_lo = lax.ppermute(tangent, "space", up)
    tan_hi = lax.ppermute(tangent, "space", down)
    tensors = (pos_rows, tangent, tan_lo, tan_hi)
    grad = pl.pallas_call(
        grad_kernel,
        grid_spec=pltpu.PrefetchScalarGridSpec(
            num_scalar_prefetch=2,
            grid=(owned // STEP_BLOCKS,),
            in_specs=[whole(t) for t in tensors] + [stepped((slots, rows, rows))] * 2,
            out_specs=stepped((dims, rows)),
            scratch_shapes=[pltpu.VMEM((3 * owned, rows, 2 * TILE), jnp.bfloat16)],
        ),
        out_shape=small,
        name="variance_gradient",
    )(index, nbr_count, *tensors, first, second)
    return (mean_force, member_sum(grad))


def solution(mesh):
    return jax.shard_map(
        body,
        mesh=mesh,
        in_specs=(
            P("space", None, None),
            P("space", None, None),
            P("space", None),
            P("space"),
            P("member", None, None),
            P("member", None, None),
            P("member", None),
        ),
        out_specs=(P("space", None, None), P("space", None, None)),
        check_vma=False,
    )
```

```python
import math

import jax
import jax.numpy as jnp
from jax import lax
from jax.experimental import pallas as pl
from jax.experimental.pallas import tpu as pltpu
from jax.sharding import PartitionSpec as P

STEP_BLOCKS = 4
CHUNK = 32
PIECES = 3
TILE = 16
LOG2E = 1.4426950408889634


def ring(axis, shift):
    count = lax.axis_size(axis)
    return [(i, (i + shift) % count) for i in range(count)]


def flip(axis, bit):
    return [(i, i ^ bit) for i in range(lax.axis_size(axis))]


def place(rows, row, value):
    at = lax.broadcasted_iota(jnp.int32, rows.shape, 0) == row
    return jnp.where(at, value, rows)


def pattern(depth, base, axis, width, value):
    row = lax.broadcasted_iota(jnp.int32, (depth, width), 0)
    hit = row == base + axis
    for piece in range(1, PIECES):
        hit = hit | (row == base + 3 * piece + axis)
    return jnp.where(hit, value, 0.0)


def difference_rhs(rows, axis, depth):
    rhs = pattern(depth, 0, axis, rows.shape[1], -1.0)
    for piece in range(PIECES):
        at = 3 * piece + axis
        rhs = place(rhs, 3 * PIECES + piece, rows[at:at + 1])
    return rhs.astype(jnp.bfloat16)


def change_rhs(pieces, axis, depth):
    rhs = pattern(depth, TILE, axis, pieces[0].shape[1], 1.0)
    for piece in range(PIECES):
        rhs = place(rhs, 3 * PIECES + piece, -pieces[piece][axis:axis + 1])
    return rhs.astype(jnp.bfloat16)


def split(array):
    pieces = []
    rest = array
    for _ in range(PIECES):
        piece = rest.astype(jnp.bfloat16).astype(jnp.float32)
        pieces.append(piece)
        rest = rest - piece
    return pieces


def pair_kernel(
    idx_ref, cnt_ref, rate_ref, core_ref,
    own_ref, lo_a, lo_b, hi_a, hi_b, embed_ref, wproj_ref,
    force_ref, first_ref, second_ref, rows_ref,
    proj_ref, col_ref,
):
    owned = own_ref.shape[0]
    half = lo_a.shape[0]
    slots = first_ref.shape[1]
    rows = first_ref.shape[2]
    channels = own_ref.shape[2]
    bases = wproj_ref.shape[1] // channels
    escale = 1.0 / math.sqrt(slots * rows)
    sigma = 1.0 / math.sqrt(channels)
    step = pl.program_id(0)

    @pl.when(step == 0)
    def _():
        def project(source, base):
            def one(i, carry):
                x = source[pl.ds(2 * i, 2), pl.ds(0, rows), :].reshape(2 * rows, channels)
                h = jnp.dot(x, embed_ref[...], preferred_element_type=jnp.float32)
                half_h = 0.5 * h
                hidden = (half_h + half_h * jnp.tanh(half_h)).astype(jnp.bfloat16)
                out = jnp.dot(hidden, wproj_ref[...], preferred_element_type=jnp.float32)
                proj_ref[pl.ds(base + 2 * i, 2)] = out.astype(jnp.bfloat16).reshape(2, rows, bases * channels)
                for j in range(2):
                    tile = source[2 * i + j, pl.ds(rows, TILE), :]
                    rows_ref[base + 2 * i + j] = tile
                    col_ref[base + 2 * i + j] = jnp.transpose(tile.astype(jnp.float32)).astype(jnp.bfloat16)
                return carry

            lax.fori_loop(0, source.shape[0] // 2, one, 0, unroll=2)

        near = core_ref[0] * half
        far = half - near
        project(own_ref, owned)
        project(lo_a, near)
        project(lo_b, far)
        project(hi_a, 2 * owned + near)
        project(hi_b, 2 * owned + far)

    decay = [-LOG2E * rate_ref[k] for k in range(bases)]
    slope_coef = [(-2.0 * sigma) * rate_ref[k] for k in range(bases)]
    bend_coef = [(4.0 * sigma) * rate_ref[k] * rate_ref[k] for k in range(bases)]

    def one_block(part, carry):
        block = step * STEP_BLOCKS + part
        count = cnt_ref[block]

        def run(live):
            left = proj_ref[owned + block]
            tile = own_ref[block, pl.ds(rows, TILE), :].astype(jnp.float32)
            separators = [difference_rhs(tile, a, TILE) for a in range(3)]
            total = [jnp.zeros((8, rows), jnp.float32) for _ in range(3)]
            for slot in range(live):
                source = idx_ref[block * slots + slot]
                cols = col_ref[source]
                parts = [jnp.dot(cols, r, preferred_element_type=jnp.float32) for r in separators]
                dots = [
                    lax.dot_general(
                        proj_ref[source, :, k * channels:(k + 1) * channels],
                        left[:, k * channels:(k + 1) * channels],
                        (((1,), (1,)), ((), ())),
                        preferred_element_type=jnp.float32,
                    )
                    for k in range(bases)
                ]
                for start in range(0, rows, CHUNK):
                    delta = [p[start:start + CHUNK] for p in parts]
                    square = delta[0] * delta[0] + delta[1] * delta[1] + delta[2] * delta[2]
                    w = [
                        jnp.exp2(decay[k] * square) * dots[k][start:start + CHUNK]
                        for k in range(bases)
                    ]
                    lh = (0.5 * sigma) * sum(w[1:], w[0])
                    slope = sum([slope_coef[k] * w[k] for k in range(1, bases)], slope_coef[0] * w[0])
                    bend = sum([bend_coef[k] * w[k] for k in range(1, bases)], bend_coef[0] * w[0])
                    h = jnp.tanh(lh)
                    u = 1.0 - h * h
                    p1 = (1.0 + h) + lh * u
                    p2 = u * (1.0 - lh * h)
                    first = p1 * slope
                    second = p2 * (slope * slope) + p1 * bend
                    first_ref[part, slot, start:start + CHUNK, :] = first
                    second_ref[part, slot, start:start + CHUNK, :] = second
                    for a in range(3):
                        total[a] = total[a] + jnp.sum((first * delta[a]).reshape(CHUNK // 8, 8, rows), axis=0)
            force_ref[part] = jnp.concatenate(
                [(-0.5 * escale) * jnp.sum(t, axis=0, keepdims=True) for t in total], axis=0
            )

        for live in range(3, slots + 1):
            pl.when(count == live)(lambda live=live: run(live))
        return carry

    lax.fori_loop(0, STEP_BLOCKS, one_block, 0)


def grad_kernel(
    idx_ref, cnt_ref, pos_ref, tan_own, tan_lo, tan_hi, first_ref, second_ref,
    grad_ref, col_ref,
):
    owned = tan_own.shape[0]
    slots = first_ref.shape[1]
    rows = first_ref.shape[2]
    escale = 1.0 / math.sqrt(slots * rows)
    step = pl.program_id(0)

    @pl.when(step == 0)
    def _():
        def spread(tan, base):
            def one(i, carry):
                filler = jnp.zeros((TILE - 3 * PIECES, rows), jnp.float32)
                tile = jnp.concatenate(
                    [pos_ref[base + i].astype(jnp.float32)] + split(tan[i]) + [filler], axis=0
                )
                col_ref[base + i] = jnp.transpose(tile).astype(jnp.bfloat16)
                return carry

            lax.fori_loop(0, owned, one, 0, unroll=4)

        spread(tan_lo, 0)
        spread(tan_own, owned)
        spread(tan_hi, 2 * owned)

    def one_block(part, carry):
        block = step * STEP_BLOCKS + part
        count = cnt_ref[block]

        def run(live):
            tile = pos_ref[owned + block].astype(jnp.float32)
            pieces = split(tan_own[block])
            sides = [difference_rhs(tile, a, 2 * TILE) for a in range(3)]
            sides += [change_rhs(pieces, a, 2 * TILE) for a in range(3)]
            total = [jnp.zeros((8, rows), jnp.float32) for _ in range(3)]
            for slot in range(live):
                source = idx_ref[block * slots + slot]
                cols = col_ref[source]
                parts = [jnp.dot(cols, r, preferred_element_type=jnp.float32) for r in sides]
                for start in range(0, rows, CHUNK):
                    delta = [p[start:start + CHUNK] for p in parts[:3]]
                    change = [p[start:start + CHUNK] for p in parts[3:]]
                    first = first_ref[part, slot, start:start + CHUNK, :]
                    second = second_ref[part, slot, start:start + CHUNK, :]
                    along = second * (delta[0] * change[0] + delta[1] * change[1] + delta[2] * change[2])
                    for a in range(3):
                        term = first * change[a] + along * delta[a]
                        total[a] = total[a] + jnp.sum(term.reshape(CHUNK // 8, 8, rows), axis=0)
            grad_ref[part] = jnp.concatenate(
                [(0.5 * escale) * jnp.sum(t, axis=0, keepdims=True) for t in total], axis=0
            )

        for live in range(3, slots + 1):
            pl.when(count == live)(lambda live=live: run(live))
        return carry

    lax.fori_loop(0, STEP_BLOCKS, one_block, 0)


def pack(features, positions):
    blocks, dims, rows = positions.shape
    pieces = []
    rest = positions
    for _ in range(PIECES):
        piece = lax.reduce_precision(rest, 8, 7)
        pieces.append(piece.astype(jnp.bfloat16))
        rest = rest - piece
    ones = jnp.ones((blocks, PIECES, rows), jnp.bfloat16)
    zeros = jnp.zeros((blocks, TILE - PIECES * (dims + 1), rows), jnp.bfloat16)
    return jnp.concatenate([features] + pieces + [ones, zeros], axis=1)


def whole(array):
    return pl.BlockSpec(array.shape, lambda *_: (0,) * len(array.shape), pipeline_mode=pl.Buffered(1))


def stepped(shape):
    return pl.BlockSpec((STEP_BLOCKS,) + shape, lambda i, *_: (i,) + (0,) * len(shape))


def member_sum(array):
    size = lax.axis_size("member")
    others = [lax.ppermute(array, "member", flip("member", bit)) for bit in range(1, size)]
    return array + others[0] + (others[1] + others[2])


def body(positions, features, nbr_list, nbr_count, w_embed, w_proj, rates):
    owned, dims, rows = positions.shape
    channels = features.shape[2]
    slots = nbr_list.shape[1]
    width = w_proj.shape[2]
    domains = lax.axis_size("space")
    members = lax.axis_size("member")
    domain = lax.axis_index("space")
    core = lax.axis_index("member") % 2
    up, down = ring("space", 1), ring("space", -1)
    half = owned // 2

    packed = pack(features, positions)
    mine = lax.dynamic_slice_in_dim(packed, core * half, half, 0)
    lo_a = lax.ppermute(mine, "space", up)
    hi_a = lax.ppermute(mine, "space", down)
    swap = flip("member", 1)
    lo_b = lax.ppermute(lo_a, "member", swap)
    hi_b = lax.ppermute(hi_a, "member", swap)

    index = jnp.mod(nbr_list - (domain - 1) * owned, domains * owned).reshape(-1)
    core_arr = core.astype(jnp.int32).reshape(1)
    pairs = jax.ShapeDtypeStruct((owned, slots, rows, rows), jnp.float32)
    small = jax.ShapeDtypeStruct((owned, dims, rows), jnp.float32)
    tensors = (packed, lo_a, lo_b, hi_a, hi_b, w_embed[0], w_proj[0])
    tiles = jax.ShapeDtypeStruct((3 * owned, TILE, rows), jnp.bfloat16)
    force, first, second, pos_rows = pl.pallas_call(
        pair_kernel,
        grid_spec=pltpu.PrefetchScalarGridSpec(
            num_scalar_prefetch=4,
            grid=(owned // STEP_BLOCKS,),
            in_specs=[whole(t) for t in tensors],
            out_specs=[stepped((dims, rows)), stepped((slots, rows, rows)), stepped((slots, rows, rows)), whole(tiles)],
            scratch_shapes=[
                pltpu.VMEM((3 * owned, rows, width), jnp.bfloat16),
                pltpu.VMEM((3 * owned, rows, TILE), jnp.bfloat16),
            ],
        ),
        out_shape=[small, pairs, pairs, tiles],
        compiler_params=pltpu.CompilerParams(vmem_limit_bytes=26 << 20),
        name="pair_forces",
    )(index, nbr_count, rates[0], core_arr, *tensors)

    mean_force = member_sum(force) / members
    tangent = (2.0 / members) * (force - mean_force)
    tan_lo = lax.ppermute(tangent, "space", up)
    tan_hi = lax.ppermute(tangent, "space", down)
    tensors = (pos_rows, tangent, tan_lo, tan_hi)
    grad = pl.pallas_call(
        grad_kernel,
        grid_spec=pltpu.PrefetchScalarGridSpec(
            num_scalar_prefetch=2,
            grid=(owned // STEP_BLOCKS,),
            in_specs=[whole(t) for t in tensors] + [stepped((slots, rows, rows))] * 2,
            out_specs=stepped((dims, rows)),
            scratch_shapes=[pltpu.VMEM((3 * owned, rows, 2 * TILE), jnp.bfloat16)],
        ),
        out_shape=small,
        compiler_params=pltpu.CompilerParams(vmem_limit_bytes=14 << 20),
        name="variance_gradient",
    )(index, nbr_count, *tensors, first, second)
    return (mean_force, member_sum(grad))


def solution(mesh):
    return jax.shard_map(
        body,
        mesh=mesh,
        in_specs=(
            P("space", None, None),
            P("space", None, None),
            P("space", None),
            P("space"),
            P("member", None, None),
            P("member", None, None),
            P("member", None),
        ),
        out_specs=(P("space", None, None), P("space", None, None)),
        check_vma=False,
    )
```

```python
import functools
import math

import jax
import jax.numpy as jnp
from jax import lax
from jax.experimental import pallas as pl
from jax.experimental.pallas import tpu as pltpu
from jax.sharding import PartitionSpec as P

STEP_BLOCKS = 4
CHUNK = 32
PIECES = 3
TILE = 16
LOG2E = 1.4426950408889634


def ring(axis, shift):
    count = lax.axis_size(axis)
    return [(i, (i + shift) % count) for i in range(count)]


def flip(axis, bit):
    return [(i, i ^ bit) for i in range(lax.axis_size(axis))]


def place(rows, row, value):
    at = lax.broadcasted_iota(jnp.int32, rows.shape, 0) == row
    return jnp.where(at, value, rows)


def pattern(depth, base, axis, width, value):
    row = lax.broadcasted_iota(jnp.int32, (depth, width), 0)
    hit = row == base + axis
    for piece in range(1, PIECES):
        hit = hit | (row == base + 3 * piece + axis)
    return jnp.where(hit, value, 0.0)


def difference_rhs(rows, axis, depth):
    rhs = pattern(depth, 0, axis, rows.shape[1], -1.0)
    for piece in range(PIECES):
        at = 3 * piece + axis
        rhs = place(rhs, 3 * PIECES + piece, rows[at:at + 1])
    return rhs.astype(jnp.bfloat16)


def change_rhs(pieces, axis, depth):
    rhs = pattern(depth, TILE, axis, pieces[0].shape[1], 1.0)
    for piece in range(PIECES):
        rhs = place(rhs, 3 * PIECES + piece, -pieces[piece][axis:axis + 1])
    return rhs.astype(jnp.bfloat16)


def split(array):
    pieces = []
    rest = array
    for _ in range(PIECES):
        piece = rest.astype(jnp.bfloat16).astype(jnp.float32)
        pieces.append(piece)
        rest = rest - piece
    return pieces


def coefficients(rate_ref, bases, sigma):
    rate = [rate_ref[k] for k in range(bases)]
    decay = [-LOG2E * r for r in rate]
    slope = [(-2.0 * sigma) * r for r in rate]
    bend = [(4.0 * sigma) * r * r for r in rate]
    return decay, slope, bend


def pair_terms(delta, dots, coefs, sigma):
    decay, slope_coef, bend_coef = coefs
    bases = len(dots)
    square = delta[0] * delta[0] + delta[1] * delta[1] + delta[2] * delta[2]
    w = [jnp.exp2(decay[k] * square) * dots[k] for k in range(bases)]
    lh = (0.5 * sigma) * sum(w[1:], w[0])
    slope = sum([slope_coef[k] * w[k] for k in range(1, bases)], slope_coef[0] * w[0])
    bend = sum([bend_coef[k] * w[k] for k in range(1, bases)], bend_coef[0] * w[0])
    h = jnp.tanh(lh)
    u = 1.0 - h * h
    p1 = (1.0 + h) + lh * u
    p2 = u * (1.0 - lh * h)
    return p1 * slope, p2 * (slope * slope) + p1 * bend


def slot_terms(right, left, cols, separators, coefs, sigma, total, store):
    channels = left.shape[1] // len(coefs[0])
    rows = left.shape[0]
    parts = [jnp.dot(cols, r, preferred_element_type=jnp.float32) for r in separators]
    dots = [
        lax.dot_general(
            right[:, k * channels:(k + 1) * channels],
            left[:, k * channels:(k + 1) * channels],
            (((1,), (1,)), ((), ())),
            preferred_element_type=jnp.float32,
        )
        for k in range(len(coefs[0]))
    ]
    for start in range(0, rows, CHUNK):
        delta = [p[start:start + CHUNK] for p in parts]
        first, second = pair_terms(delta, [d[start:start + CHUNK] for d in dots], coefs, sigma)
        store(start, first, second)
        for a in range(3):
            total[a] = total[a] + jnp.sum((first * delta[a]).reshape(CHUNK // 8, 8, rows), axis=0)


def gather_rows(total, factor):
    return jnp.concatenate([factor * jnp.sum(t, axis=0, keepdims=True) for t in total], axis=0)


def project(x, embed_ref, wproj_ref):
    h = jnp.dot(x, embed_ref[...], preferred_element_type=jnp.float32)
    half_h = 0.5 * h
    hidden = (half_h + half_h * jnp.tanh(half_h)).astype(jnp.bfloat16)
    out = jnp.dot(hidden, wproj_ref[...], preferred_element_type=jnp.float32)
    return out.astype(jnp.bfloat16)


def own_kernel(slots, rate_ref, own_ref, pos_ref, embed_ref, wproj_ref,
               force_ref, first_ref, second_ref, tile_ref, proj_ref):
    rows, channels = own_ref.shape[1:]
    bases = wproj_ref.shape[1] // channels
    escale = 1.0 / math.sqrt(slots * rows)
    sigma = 1.0 / math.sqrt(channels)
    coefs = coefficients(rate_ref, bases, sigma)
    flat = own_ref[...].reshape(STEP_BLOCKS * rows, channels)
    proj_ref[...] = project(flat, embed_ref, wproj_ref).reshape(STEP_BLOCKS, rows, bases * channels)
    for part in range(STEP_BLOCKS):
        ones = jnp.ones((PIECES, rows), jnp.float32)
        zeros = jnp.zeros((TILE - 4 * PIECES, rows), jnp.float32)
        tile = jnp.concatenate(split(pos_ref[part]) + [ones, zeros], axis=0)
        tile_ref[part] = tile.astype(jnp.bfloat16)
        cols = jnp.transpose(tile).astype(jnp.bfloat16)
        separators = [difference_rhs(tile, a, TILE) for a in range(3)]
        total = [jnp.zeros((8, rows), jnp.float32) for _ in range(3)]

        def store(start, first, second, part=part):
            first_ref[part, start:start + CHUNK, :] = first
            second_ref[part, start:start + CHUNK, :] = second

        left = proj_ref[part]
        slot_terms(left, left, cols, separators, coefs, sigma, total, store)
        force_ref[part] = gather_rows(total, -0.5 * escale)


def pair_kernel(
    nbr_ref, cnt_ref, rate_ref, meta_ref,
    own_proj, lo_a, lo_b, hi_a, hi_b, embed_ref, wproj_ref, own_tile, part_ref,
    force_ref, first_ref, second_ref, rows_ref,
    proj_ref, col_ref, sem,
):
    owned = own_tile.shape[0]
    half = lo_a.shape[0]
    slots = nbr_ref.shape[1]
    rows = first_ref.shape[2]
    channels = embed_ref.shape[0]
    bases = wproj_ref.shape[1] // channels
    escale = 1.0 / math.sqrt(slots * rows)
    sigma = 1.0 / math.sqrt(channels)
    step = pl.program_id(0)

    @pl.when(step == 0)
    def _():
        copy = pltpu.make_async_copy(own_proj, proj_ref.at[pl.ds(owned, owned)], sem)
        copy.start()

        def keep(tile, at):
            rows_ref[at] = tile
            col_ref[at] = jnp.transpose(tile.astype(jnp.float32)).astype(jnp.bfloat16)

        def take(source, base):
            def one(i, carry):
                x = source[pl.ds(2 * i, 2), pl.ds(0, rows), :].reshape(2 * rows, channels)
                out = project(x, embed_ref, wproj_ref)
                proj_ref[pl.ds(base + 2 * i, 2)] = out.reshape(2, rows, bases * channels)
                for j in range(2):
                    keep(source[2 * i + j, pl.ds(rows, TILE), :], base + 2 * i + j)
                return carry

            lax.fori_loop(0, half // 2, one, 0, unroll=4)

        near = meta_ref[1] * half
        far = half - near
        take(lo_a, near)
        take(hi_a, 2 * owned + near)
        take(lo_b, far)
        take(hi_b, 2 * owned + far)

        def own(i, carry):
            keep(own_tile[i], owned + i)
            return carry

        lax.fori_loop(0, owned, own, 0, unroll=4)
        copy.wait()

    coefs = coefficients(rate_ref, bases, sigma)
    offset = meta_ref[0]
    total_blocks = meta_ref[2]

    def one_block(part, carry):
        block = step * STEP_BLOCKS + part
        count = cnt_ref[block]

        def run(live):
            left = proj_ref[owned + block]
            tile = own_tile[block].astype(jnp.float32)
            separators = [difference_rhs(tile, a, TILE) for a in range(3)]
            total = [jnp.zeros((8, rows), jnp.float32) for _ in range(3)]
            for slot in range(1, live):
                source = nbr_ref[block, slot] - offset
                source = jnp.where(source < 0, source + total_blocks, source)
                source = jnp.where(source >= total_blocks, source - total_blocks, source)

                def store(start, first, second, slot=slot):
                    first_ref[part, slot - 1, start:start + CHUNK, :] = first
                    second_ref[part, slot - 1, start:start + CHUNK, :] = second

                slot_terms(proj_ref[source], left, col_ref[source], separators, coefs, sigma, total, store)
            force_ref[part] = part_ref[part] + gather_rows(total, -0.5 * escale)

        for live in range(3, slots + 1):
            pl.when(count == live)(lambda live=live: run(live))
        return carry

    lax.fori_loop(0, STEP_BLOCKS, one_block, 0)


def grad_kernel(
    nbr_ref, cnt_ref, meta_ref, pos_ref, tan_own, tan_lo, tan_hi,
    own_first, own_second, first_ref, second_ref,
    grad_ref, col_ref,
):
    owned = tan_own.shape[0]
    slots = nbr_ref.shape[1]
    rows = first_ref.shape[2]
    escale = 1.0 / math.sqrt(slots * rows)
    step = pl.program_id(0)

    @pl.when(step == 0)
    def _():
        def spread(tan, base):
            def one(i, carry):
                filler = jnp.zeros((TILE - 3 * PIECES, rows), jnp.float32)
                tile = jnp.concatenate(
                    [pos_ref[base + i].astype(jnp.float32)] + split(tan[i]) + [filler], axis=0
                )
                col_ref[base + i] = jnp.transpose(tile).astype(jnp.bfloat16)
                return carry

            lax.fori_loop(0, owned, one, 0, unroll=4)

        spread(tan_lo, 0)
        spread(tan_own, owned)
        spread(tan_hi, 2 * owned)

    offset = meta_ref[0]
    total_blocks = meta_ref[2]

    def one_block(part, carry):
        block = step * STEP_BLOCKS + part
        count = cnt_ref[block]

        def run(live):
            tile = pos_ref[owned + block].astype(jnp.float32)
            pieces = split(tan_own[block])
            sides = [difference_rhs(tile, a, 2 * TILE) for a in range(3)]
            sides += [change_rhs(pieces, a, 2 * TILE) for a in range(3)]
            total = [jnp.zeros((8, rows), jnp.float32) for _ in range(3)]
            for slot in range(live):
                source = owned + block
                if slot:
                    source = nbr_ref[block, slot] - offset
                    source = jnp.where(source < 0, source + total_blocks, source)
                    source = jnp.where(source >= total_blocks, source - total_blocks, source)
                cols = col_ref[source]
                parts = [jnp.dot(cols, r, preferred_element_type=jnp.float32) for r in sides]
                for start in range(0, rows, CHUNK):
                    delta = [p[start:start + CHUNK] for p in parts[:3]]
                    change = [p[start:start + CHUNK] for p in parts[3:]]
                    span = slice(start, start + CHUNK)
                    first = first_ref[part, slot - 1, span, :] if slot else own_first[part, span, :]
                    second = second_ref[part, slot - 1, span, :] if slot else own_second[part, span, :]
                    along = second * (delta[0] * change[0] + delta[1] * change[1] + delta[2] * change[2])
                    for a in range(3):
                        term = first * change[a] + along * delta[a]
                        total[a] = total[a] + jnp.sum(term.reshape(CHUNK // 8, 8, rows), axis=0)
            grad_ref[part] = gather_rows(total, 0.5 * escale)

        for live in range(3, slots + 1):
            pl.when(count == live)(lambda live=live: run(live))
        return carry

    lax.fori_loop(0, STEP_BLOCKS, one_block, 0)


def pack_kernel(meta_ref, feat_ref, pos_ref, out_ref):
    blocks, rows, _ = feat_ref.shape
    out_ref[:, pl.ds(0, rows), :] = feat_ref[...]
    ones = jnp.ones((PIECES, rows), jnp.float32)
    zeros = jnp.zeros((TILE - 4 * PIECES, rows), jnp.float32)
    for i in range(blocks):
        tile = jnp.concatenate(split(pos_ref[i]) + [ones, zeros], axis=0)
        out_ref[i, pl.ds(rows, TILE), :] = tile.astype(jnp.bfloat16)


def in_hbm(array):
    return pltpu.with_memory_space_constraint(array, pltpu.HBM)


def whole(array):
    return pl.BlockSpec(array.shape, lambda *_: (0,) * len(array.shape), pipeline_mode=pl.Buffered(1))


def stepped(shape):
    return pl.BlockSpec((STEP_BLOCKS,) + shape, lambda i, *_: (i,) + (0,) * len(shape))


def member_sum(array):
    size = lax.axis_size("member")
    others = [lax.ppermute(array, "member", flip("member", bit)) for bit in range(1, size)]
    return array + others[0] + (others[1] + others[2])


def body(positions, features, nbr_list, nbr_count, w_embed, w_proj, rates):
    owned, dims, rows = positions.shape
    channels = features.shape[2]
    slots = nbr_list.shape[1]
    width = w_proj.shape[2]
    domains = lax.axis_size("space")
    members = lax.axis_size("member")
    domain = lax.axis_index("space")
    core = lax.axis_index("member") % 2
    up, down = ring("space", 1), ring("space", -1)
    half = owned // 2

    offset = (domain - 1) * owned
    meta = jnp.stack([offset, core, jnp.int32(domains * owned)]).astype(jnp.int32)
    embed, proj = in_hbm(w_embed[0]), in_hbm(w_proj[0])
    rate, counts = in_hbm(rates[0]), in_hbm(nbr_count)
    mine = pl.pallas_call(
        pack_kernel,
        grid_spec=pltpu.PrefetchScalarGridSpec(
            num_scalar_prefetch=1,
            grid=(1,),
            in_specs=[
                pl.BlockSpec((half, rows, channels), lambda i, m: (m[1], 0, 0)),
                pl.BlockSpec((half, dims, rows), lambda i, m: (m[1], 0, 0)),
            ],
            out_specs=pl.BlockSpec((half, rows + TILE, channels), lambda i, m: (0, 0, 0)),
        ),
        out_shape=jax.ShapeDtypeStruct((half, rows + TILE, channels), jnp.bfloat16),
        compiler_params=pltpu.CompilerParams(vmem_limit_bytes=8 << 20),
        name="pack_halo",
    )(meta, in_hbm(features), positions)
    lo_a = lax.ppermute(mine, "space", up)
    hi_a = lax.ppermute(mine, "space", down)
    pair = (rows, rows)
    selfs = jax.ShapeDtypeStruct((owned,) + pair, jnp.float32)
    pairs = jax.ShapeDtypeStruct((owned, slots - 1) + pair, jnp.float32)
    small = jax.ShapeDtypeStruct((owned, dims, rows), jnp.float32)
    tiles = jax.ShapeDtypeStruct((owned, TILE, rows), jnp.bfloat16)
    window = jax.ShapeDtypeStruct((3 * owned, TILE, rows), jnp.bfloat16)
    table = jax.ShapeDtypeStruct((owned, rows, width), jnp.bfloat16)
    steps = (owned // STEP_BLOCKS,)
    part_force, own_first, own_second, own_tile, own_proj = pl.pallas_call(
        functools.partial(own_kernel, slots),
        grid_spec=pltpu.PrefetchScalarGridSpec(
            num_scalar_prefetch=1,
            grid=steps,
            in_specs=[stepped((rows, channels)), stepped((dims, rows)), whole(w_embed[0]), whole(w_proj[0])],
            out_specs=[
                stepped((dims, rows)), stepped(pair), stepped(pair),
                stepped((TILE, rows)), stepped((rows, width)),
            ],
        ),
        out_shape=[small, selfs, selfs, tiles, table],
        compiler_params=pltpu.CompilerParams(vmem_limit_bytes=8 << 20),
        name="own_pairs",
    )(rate, in_hbm(features), positions, embed, proj)
    lo_a, hi_a, own_tile = lax.optimization_barrier((lo_a, hi_a, own_tile))
    swap = flip("member", 1)
    lo_b = lax.ppermute(lo_a, "member", swap)
    hi_b = lax.ppermute(hi_a, "member", swap)
    halo = (lo_a, lo_b, hi_a, hi_b, embed, proj, own_tile)
    force, first, second, pos_rows = pl.pallas_call(
        pair_kernel,
        grid_spec=pltpu.PrefetchScalarGridSpec(
            num_scalar_prefetch=4,
            grid=steps,
            in_specs=[pl.BlockSpec(memory_space=pl.ANY)] + [whole(t) for t in halo] + [stepped((dims, rows))],
            out_specs=[
                stepped((dims, rows)), stepped((slots - 1,) + pair), stepped((slots - 1,) + pair), whole(window),
            ],
            scratch_shapes=[
                pltpu.VMEM((3 * owned, rows, width), jnp.bfloat16),
                pltpu.VMEM((3 * owned, rows, TILE), jnp.bfloat16),
                pltpu.SemaphoreType.DMA,
            ],
        ),
        out_shape=[small, pairs, pairs, window],
        compiler_params=pltpu.CompilerParams(vmem_limit_bytes=18 << 20),
        name="halo_pairs",
    )(nbr_list, counts, rate, meta, own_proj, *halo, in_hbm(part_force))

    mean_force = member_sum(force) / members
    tangent = (2.0 / members) * (force - mean_force)
    tan_lo = lax.ppermute(tangent, "space", up)
    tan_hi = lax.ppermute(tangent, "space", down)
    tensors = (pos_rows, tangent, tan_lo, tan_hi)
    grad = pl.pallas_call(
        grad_kernel,
        grid_spec=pltpu.PrefetchScalarGridSpec(
            num_scalar_prefetch=3,
            grid=steps,
            in_specs=[whole(t) for t in tensors] + [stepped(pair)] * 2 + [stepped((slots - 1,) + pair)] * 2,
            out_specs=stepped((dims, rows)),
            scratch_shapes=[pltpu.VMEM((3 * owned, rows, 2 * TILE), jnp.bfloat16)],
        ),
        out_shape=small,
        compiler_params=pltpu.CompilerParams(vmem_limit_bytes=10 << 20),
        name="variance_gradient",
    )(nbr_list, counts, meta, *tensors, in_hbm(own_first), in_hbm(own_second), first, second)
    return (mean_force, member_sum(grad))


def solution(mesh):
    return jax.shard_map(
        body,
        mesh=mesh,
        in_specs=(
            P("space", None, None),
            P("space", None, None),
            P("space", None),
            P("space"),
            P("member", None, None),
            P("member", None, None),
            P("member", None),
        ),
        out_specs=(P("space", None, None), P("space", None, None)),
        check_vma=False,
    )
```

```python
import functools
import math

import jax
import jax.numpy as jnp
from jax import lax
from jax.experimental import pallas as pl
from jax.experimental.pallas import tpu as pltpu
from jax.sharding import PartitionSpec as P

STEP_BLOCKS = 4
CHUNK = 32
PIECES = 3
TILE = 16
LOG2E = 1.4426950408889634


def ring(axis, shift):
    count = lax.axis_size(axis)
    return [(i, (i + shift) % count) for i in range(count)]


def flip(axis, bit):
    return [(i, i ^ bit) for i in range(lax.axis_size(axis))]


def place(rows, row, value):
    at = lax.broadcasted_iota(jnp.int32, rows.shape, 0) == row
    return jnp.where(at, value, rows)


def pattern(depth, base, axis, width, value):
    row = lax.broadcasted_iota(jnp.int32, (depth, width), 0)
    hit = row == base + axis
    for piece in range(1, PIECES):
        hit = hit | (row == base + 3 * piece + axis)
    return jnp.where(hit, value, 0.0)


def difference_rhs(rows, axis, depth):
    rhs = pattern(depth, 0, axis, rows.shape[1], -1.0)
    for piece in range(PIECES):
        at = 3 * piece + axis
        rhs = place(rhs, 3 * PIECES + piece, rows[at:at + 1])
    return rhs.astype(jnp.bfloat16)


def change_rhs(pieces, axis, depth):
    rhs = pattern(depth, TILE, axis, pieces[0].shape[1], 1.0)
    for piece in range(PIECES):
        rhs = place(rhs, 3 * PIECES + piece, -pieces[piece][axis:axis + 1])
    return rhs.astype(jnp.bfloat16)


def split(array):
    pieces = []
    rest = array
    for _ in range(PIECES):
        piece = rest.astype(jnp.bfloat16).astype(jnp.float32)
        pieces.append(piece)
        rest = rest - piece
    return pieces


def coefficients(rate_ref, bases, sigma):
    rate = [rate_ref[k] for k in range(bases)]
    decay = [-LOG2E * r for r in rate]
    slope = [(-2.0 * sigma) * r for r in rate]
    bend = [(4.0 * sigma) * r * r for r in rate]
    return decay, slope, bend


def pair_terms(delta, dots, coefs, sigma):
    decay, slope_coef, bend_coef = coefs
    bases = len(dots)
    square = delta[0] * delta[0] + delta[1] * delta[1] + delta[2] * delta[2]
    w = [jnp.exp2(decay[k] * square) * dots[k] for k in range(bases)]
    lh = (0.5 * sigma) * sum(w[1:], w[0])
    slope = sum([slope_coef[k] * w[k] for k in range(1, bases)], slope_coef[0] * w[0])
    bend = sum([bend_coef[k] * w[k] for k in range(1, bases)], bend_coef[0] * w[0])
    h = jnp.tanh(lh)
    u = 1.0 - h * h
    p1 = (1.0 + h) + lh * u
    p2 = u * (1.0 - lh * h)
    return p1 * slope, p2 * (slope * slope) + p1 * bend


def slot_terms(right, left, cols, separators, coefs, sigma, total, store):
    channels = left.shape[1] // len(coefs[0])
    rows = left.shape[0]
    parts = [jnp.dot(cols, r, preferred_element_type=jnp.float32) for r in separators]
    dots = [
        lax.dot_general(
            right[:, k * channels:(k + 1) * channels],
            left[:, k * channels:(k + 1) * channels],
            (((1,), (1,)), ((), ())),
            preferred_element_type=jnp.float32,
        )
        for k in range(len(coefs[0]))
    ]
    for start in range(0, rows, CHUNK):
        delta = [p[start:start + CHUNK] for p in parts]
        first, second = pair_terms(delta, [d[start:start + CHUNK] for d in dots], coefs, sigma)
        store(start, first, second)
        for a in range(3):
            total[a] = total[a] + jnp.sum((first * delta[a]).reshape(CHUNK // 8, 8, rows), axis=0)


def gather_rows(total, factor):
    return jnp.concatenate([factor * jnp.sum(t, axis=0, keepdims=True) for t in total], axis=0)


def project(x, embed_ref, wproj_ref):
    h = jnp.dot(x, embed_ref[...], preferred_element_type=jnp.float32)
    half_h = 0.5 * h
    hidden = (half_h + half_h * jnp.tanh(half_h)).astype(jnp.bfloat16)
    out = jnp.dot(hidden, wproj_ref[...], preferred_element_type=jnp.float32)
    return out.astype(jnp.bfloat16)


def own_kernel(slots, rate_ref, own_ref, pos_ref, embed_ref, wproj_ref,
               force_ref, first_ref, second_ref, tile_ref, proj_ref, sep_ref):
    rows, channels = own_ref.shape[1:]
    bases = wproj_ref.shape[1] // channels
    escale = 1.0 / math.sqrt(slots * rows)
    sigma = 1.0 / math.sqrt(channels)
    coefs = coefficients(rate_ref, bases, sigma)
    flat = own_ref[...].reshape(STEP_BLOCKS * rows, channels)
    proj_ref[...] = project(flat, embed_ref, wproj_ref).reshape(STEP_BLOCKS, rows, bases * channels)
    for part in range(STEP_BLOCKS):
        ones = jnp.ones((PIECES, rows), jnp.float32)
        zeros = jnp.zeros((TILE - 4 * PIECES, rows), jnp.float32)
        tile = jnp.concatenate(split(pos_ref[part]) + [ones, zeros], axis=0)
        tile_ref[part] = tile.astype(jnp.bfloat16)
        cols = jnp.transpose(tile).astype(jnp.bfloat16)
        separators = [difference_rhs(tile, a, TILE) for a in range(3)]
        for a in range(3):
            sep_ref[part, a] = separators[a]
        total = [jnp.zeros((8, rows), jnp.float32) for _ in range(3)]

        def store(start, first, second, part=part):
            first_ref[part, start:start + CHUNK, :] = first
            second_ref[part, start:start + CHUNK, :] = second

        left = proj_ref[part]
        slot_terms(left, left, cols, separators, coefs, sigma, total, store)
        force_ref[part] = gather_rows(total, -0.5 * escale)


def pair_kernel(
    nbr_ref, cnt_ref, rate_ref, meta_ref,
    own_proj, lo_a, lo_b, hi_a, hi_b, embed_ref, wproj_ref, own_tile, part_ref, sep_ref,
    force_ref, first_ref, second_ref, rows_ref,
    proj_ref, col_ref, sem,
):
    owned = own_tile.shape[0]
    half = lo_a.shape[0]
    slots = nbr_ref.shape[1]
    rows = first_ref.shape[2]
    channels = embed_ref.shape[0]
    bases = wproj_ref.shape[1] // channels
    escale = 1.0 / math.sqrt(slots * rows)
    sigma = 1.0 / math.sqrt(channels)
    step = pl.program_id(0)

    @pl.when(step == 0)
    def _():
        copy = pltpu.make_async_copy(own_proj, proj_ref.at[pl.ds(owned, owned)], sem)
        copy.start()

        def keep(tile, at):
            rows_ref[at] = tile
            col_ref[at] = jnp.transpose(tile.astype(jnp.float32)).astype(jnp.bfloat16)

        def take(source, base):
            def one(i, carry):
                x = source[pl.ds(2 * i, 2), pl.ds(0, rows), :].reshape(2 * rows, channels)
                out = project(x, embed_ref, wproj_ref)
                proj_ref[pl.ds(base + 2 * i, 2)] = out.reshape(2, rows, bases * channels)
                for j in range(2):
                    keep(source[2 * i + j, pl.ds(rows, TILE), :], base + 2 * i + j)
                return carry

            lax.fori_loop(0, half // 2, one, 0, unroll=4)

        near = meta_ref[1] * half
        far = half - near
        take(lo_a, near)
        take(hi_a, 2 * owned + near)
        take(lo_b, far)
        take(hi_b, 2 * owned + far)

        def own(i, carry):
            keep(own_tile[i], owned + i)
            return carry

        lax.fori_loop(0, owned, own, 0, unroll=4)
        copy.wait()

    coefs = coefficients(rate_ref, bases, sigma)
    offset = meta_ref[0]
    total_blocks = meta_ref[2]

    def one_block(part, carry):
        block = step * STEP_BLOCKS + part
        count = cnt_ref[block]

        def run(live):
            left = proj_ref[owned + block]
            separators = [sep_ref[part, a] for a in range(3)]
            total = [jnp.zeros((8, rows), jnp.float32) for _ in range(3)]
            for slot in range(1, live):
                source = nbr_ref[block, slot] - offset
                source = jnp.where(source < 0, source + total_blocks, source)
                source = jnp.where(source >= total_blocks, source - total_blocks, source)

                def store(start, first, second, slot=slot):
                    first_ref[part, slot - 1, start:start + CHUNK, :] = first
                    second_ref[part, slot - 1, start:start + CHUNK, :] = second

                slot_terms(proj_ref[source], left, col_ref[source], separators, coefs, sigma, total, store)
            force_ref[part] = part_ref[part] + gather_rows(total, -0.5 * escale)

        for live in range(3, slots + 1):
            pl.when(count == live)(lambda live=live: run(live))
        return carry

    lax.fori_loop(0, STEP_BLOCKS, one_block, 0)


def grad_slot(cols, sides, first_of, second_of, total):
    rows = cols.shape[0]
    parts = [jnp.dot(cols, r, preferred_element_type=jnp.float32) for r in sides]
    for start in range(0, rows, CHUNK):
        span = slice(start, start + CHUNK)
        delta = [p[span] for p in parts[:3]]
        change = [p[span] for p in parts[3:]]
        first = first_of(span)
        along = second_of(span) * (delta[0] * change[0] + delta[1] * change[1] + delta[2] * change[2])
        for a in range(3):
            term = first * change[a] + along * delta[a]
            total[a] = total[a] + jnp.sum(term.reshape(CHUNK // 8, 8, rows), axis=0)


def tangent_columns(tile, pieces):
    filler = jnp.zeros((TILE - 3 * PIECES, tile.shape[1]), jnp.float32)
    return jnp.transpose(jnp.concatenate([tile] + pieces + [filler], axis=0)).astype(jnp.bfloat16)


def own_grad_kernel(slots, tile_ref, tan_ref, first_ref, second_ref, grad_ref, side_ref):
    rows = first_ref.shape[1]
    escale = 1.0 / math.sqrt(slots * rows)
    for part in range(STEP_BLOCKS):
        tile = tile_ref[part].astype(jnp.float32)
        pieces = split(tan_ref[part])
        sides = [difference_rhs(tile, a, 2 * TILE) for a in range(3)]
        sides += [change_rhs(pieces, a, 2 * TILE) for a in range(3)]
        for n in range(6):
            side_ref[part, n] = sides[n]
        total = [jnp.zeros((8, rows), jnp.float32) for _ in range(3)]
        grad_slot(
            tangent_columns(tile, pieces), sides,
            lambda span, part=part: first_ref[part, span, :],
            lambda span, part=part: second_ref[part, span, :],
            total,
        )
        grad_ref[part] = gather_rows(total, 0.5 * escale)


def grad_kernel(
    nbr_ref, cnt_ref, meta_ref, pos_ref, tan_own, tan_lo, tan_hi,
    part_ref, side_ref, first_ref, second_ref,
    grad_ref, col_ref,
):
    owned = tan_own.shape[0]
    slots = nbr_ref.shape[1]
    rows = first_ref.shape[2]
    escale = 1.0 / math.sqrt(slots * rows)
    step = pl.program_id(0)

    @pl.when(step == 0)
    def _():
        def spread(tan, base):
            def one(i, carry):
                col_ref[base + i] = tangent_columns(pos_ref[base + i].astype(jnp.float32), split(tan[i]))
                return carry

            lax.fori_loop(0, owned, one, 0, unroll=4)

        spread(tan_lo, 0)
        spread(tan_own, owned)
        spread(tan_hi, 2 * owned)

    offset = meta_ref[0]
    total_blocks = meta_ref[2]

    def one_block(part, carry):
        block = step * STEP_BLOCKS + part
        count = cnt_ref[block]

        def run(live):
            sides = [side_ref[part, n] for n in range(6)]
            total = [jnp.zeros((8, rows), jnp.float32) for _ in range(3)]
            for slot in range(1, live):
                source = nbr_ref[block, slot] - offset
                source = jnp.where(source < 0, source + total_blocks, source)
                source = jnp.where(source >= total_blocks, source - total_blocks, source)
                grad_slot(
                    col_ref[source], sides,
                    lambda span, slot=slot: first_ref[part, slot - 1, span, :],
                    lambda span, slot=slot: second_ref[part, slot - 1, span, :],
                    total,
                )
            grad_ref[part] = part_ref[part] + gather_rows(total, 0.5 * escale)

        for live in range(3, slots + 1):
            pl.when(count == live)(lambda live=live: run(live))
        return carry

    lax.fori_loop(0, STEP_BLOCKS, one_block, 0)


def pack_kernel(meta_ref, feat_ref, pos_ref, out_ref):
    blocks, rows, _ = feat_ref.shape
    out_ref[:, pl.ds(0, rows), :] = feat_ref[...]
    ones = jnp.ones((PIECES, rows), jnp.float32)
    zeros = jnp.zeros((TILE - 4 * PIECES, rows), jnp.float32)
    for i in range(blocks):
        tile = jnp.concatenate(split(pos_ref[i]) + [ones, zeros], axis=0)
        out_ref[i, pl.ds(rows, TILE), :] = tile.astype(jnp.bfloat16)


def in_hbm(array):
    return pltpu.with_memory_space_constraint(array, pltpu.HBM)


def whole(array):
    return pl.BlockSpec(array.shape, lambda *_: (0,) * len(array.shape), pipeline_mode=pl.Buffered(1))


def stepped(shape):
    return pl.BlockSpec((STEP_BLOCKS,) + shape, lambda i, *_: (i,) + (0,) * len(shape))


def member_sum(array):
    size = lax.axis_size("member")
    others = [lax.ppermute(array, "member", flip("member", bit)) for bit in range(1, size)]
    return array + others[0] + (others[1] + others[2])


def body(positions, features, nbr_list, nbr_count, w_embed, w_proj, rates):
    owned, dims, rows = positions.shape
    channels = features.shape[2]
    slots = nbr_list.shape[1]
    width = w_proj.shape[2]
    domains = lax.axis_size("space")
    members = lax.axis_size("member")
    domain = lax.axis_index("space")
    core = lax.axis_index("member") % 2
    up, down = ring("space", 1), ring("space", -1)
    half = owned // 2

    offset = (domain - 1) * owned
    meta = jnp.stack([offset, core, jnp.int32(domains * owned)]).astype(jnp.int32)
    embed, proj = in_hbm(w_embed[0]), in_hbm(w_proj[0])
    rate, counts = in_hbm(rates[0]), in_hbm(nbr_count)
    mine = pl.pallas_call(
        pack_kernel,
        grid_spec=pltpu.PrefetchScalarGridSpec(
            num_scalar_prefetch=1,
            grid=(1,),
            in_specs=[
                pl.BlockSpec((half, rows, channels), lambda i, m: (m[1], 0, 0)),
                pl.BlockSpec((half, dims, rows), lambda i, m: (m[1], 0, 0)),
            ],
            out_specs=pl.BlockSpec((half, rows + TILE, channels), lambda i, m: (0, 0, 0)),
        ),
        out_shape=jax.ShapeDtypeStruct((half, rows + TILE, channels), jnp.bfloat16),
        compiler_params=pltpu.CompilerParams(vmem_limit_bytes=8 << 20),
        name="pack_halo",
    )(meta, in_hbm(features), positions)
    lo_a = lax.ppermute(mine, "space", up)
    hi_a = lax.ppermute(mine, "space", down)
    pair = (rows, rows)
    selfs = jax.ShapeDtypeStruct((owned,) + pair, jnp.float32)
    pairs = jax.ShapeDtypeStruct((owned, slots - 1) + pair, jnp.float32)
    small = jax.ShapeDtypeStruct((owned, dims, rows), jnp.float32)
    tiles = jax.ShapeDtypeStruct((owned, TILE, rows), jnp.bfloat16)
    window = jax.ShapeDtypeStruct((3 * owned, TILE, rows), jnp.bfloat16)
    table = jax.ShapeDtypeStruct((owned, rows, width), jnp.bfloat16)
    separate = jax.ShapeDtypeStruct((owned, dims, TILE, rows), jnp.bfloat16)
    sides = jax.ShapeDtypeStruct((owned, 2 * dims, 2 * TILE, rows), jnp.bfloat16)
    steps = (owned // STEP_BLOCKS,)
    part_force, own_first, own_second, own_tile, own_proj, separators = pl.pallas_call(
        functools.partial(own_kernel, slots),
        grid_spec=pltpu.PrefetchScalarGridSpec(
            num_scalar_prefetch=1,
            grid=steps,
            in_specs=[stepped((rows, channels)), stepped((dims, rows)), whole(w_embed[0]), whole(w_proj[0])],
            out_specs=[
                stepped((dims, rows)), stepped(pair), stepped(pair),
                stepped((TILE, rows)), stepped((rows, width)), stepped((dims, TILE, rows)),
            ],
        ),
        out_shape=[small, selfs, selfs, tiles, table, separate],
        compiler_params=pltpu.CompilerParams(vmem_limit_bytes=8 << 20),
        name="own_pairs",
    )(rate, in_hbm(features), positions, embed, proj)
    lo_a, hi_a, own_tile = lax.optimization_barrier((lo_a, hi_a, own_tile))
    swap = flip("member", 1)
    lo_b = lax.ppermute(lo_a, "member", swap)
    hi_b = lax.ppermute(hi_a, "member", swap)
    halo = (lo_a, lo_b, hi_a, hi_b, embed, proj, own_tile)
    force, first, second, pos_rows = pl.pallas_call(
        pair_kernel,
        grid_spec=pltpu.PrefetchScalarGridSpec(
            num_scalar_prefetch=4,
            grid=steps,
            in_specs=[pl.BlockSpec(memory_space=pl.ANY)] + [whole(t) for t in halo] + [stepped((dims, rows)), stepped((dims, TILE, rows))],
            out_specs=[
                stepped((dims, rows)), stepped((slots - 1,) + pair), stepped((slots - 1,) + pair), whole(window),
            ],
            scratch_shapes=[
                pltpu.VMEM((3 * owned, rows, width), jnp.bfloat16),
                pltpu.VMEM((3 * owned, rows, TILE), jnp.bfloat16),
                pltpu.SemaphoreType.DMA,
            ],
        ),
        out_shape=[small, pairs, pairs, window],
        compiler_params=pltpu.CompilerParams(vmem_limit_bytes=18 << 20),
        name="halo_pairs",
    )(nbr_list, counts, rate, meta, own_proj, *halo, in_hbm(part_force), separators)

    mean_force = member_sum(force) / members
    tangent = (2.0 / members) * (force - mean_force)
    tan_lo = lax.ppermute(tangent, "space", up)
    tan_hi = lax.ppermute(tangent, "space", down)
    part_grad, side_table = pl.pallas_call(
        functools.partial(own_grad_kernel, slots),
        grid=steps,
        in_specs=[stepped((TILE, rows)), stepped((dims, rows)), stepped(pair), stepped(pair)],
        out_specs=[stepped((dims, rows)), stepped((2 * dims, 2 * TILE, rows))],
        out_shape=[small, sides],
        compiler_params=pltpu.CompilerParams(vmem_limit_bytes=8 << 20),
        name="own_gradient",
    )(own_tile, tangent, in_hbm(own_first), in_hbm(own_second))
    tensors = (pos_rows, tangent, tan_lo, tan_hi)
    grad = pl.pallas_call(
        grad_kernel,
        grid_spec=pltpu.PrefetchScalarGridSpec(
            num_scalar_prefetch=3,
            grid=steps,
            in_specs=[whole(t) for t in tensors] + [stepped((dims, rows)), stepped((2 * dims, 2 * TILE, rows))] + [stepped((slots - 1,) + pair)] * 2,
            out_specs=stepped((dims, rows)),
            scratch_shapes=[pltpu.VMEM((3 * owned, rows, 2 * TILE), jnp.bfloat16)],
        ),
        out_shape=small,
        compiler_params=pltpu.CompilerParams(vmem_limit_bytes=10 << 20),
        name="variance_gradient",
    )(nbr_list, counts, meta, *tensors, part_grad, side_table, first, second)
    return (mean_force, member_sum(grad))


def solution(mesh):
    return jax.shard_map(
        body,
        mesh=mesh,
        in_specs=(
            P("space", None, None),
            P("space", None, None),
            P("space", None),
            P("space"),
            P("member", None, None),
            P("member", None, None),
            P("member", None),
        ),
        out_specs=(P("space", None, None), P("space", None, None)),
        check_vma=False,
    )
```

```python
import functools
import math

import jax
import jax.numpy as jnp
from jax import lax
from jax.experimental import pallas as pl
from jax.experimental.pallas import tpu as pltpu
from jax.sharding import PartitionSpec as P

STEP_BLOCKS = 4
PAIR_BLOCKS = 2
CHUNK = 32
PIECES = 3
TILE = 16
LOG2E = 1.4426950408889634


def ring(axis, shift):
    count = lax.axis_size(axis)
    return [(i, (i + shift) % count) for i in range(count)]


def flip(axis, bit):
    return [(i, i ^ bit) for i in range(lax.axis_size(axis))]


def place(rows, row, value):
    at = lax.broadcasted_iota(jnp.int32, rows.shape, 0) == row
    return jnp.where(at, value, rows)


def pattern(depth, base, axis, width, value):
    row = lax.broadcasted_iota(jnp.int32, (depth, width), 0)
    hit = row == base + axis
    for piece in range(1, PIECES):
        hit = hit | (row == base + 3 * piece + axis)
    return jnp.where(hit, value, 0.0)


def difference_rhs(rows, axis, depth):
    rhs = pattern(depth, 0, axis, rows.shape[1], -1.0)
    for piece in range(PIECES):
        at = 3 * piece + axis
        rhs = place(rhs, 3 * PIECES + piece, rows[at:at + 1])
    return rhs.astype(jnp.bfloat16)


def change_rhs(pieces, axis, depth):
    rhs = pattern(depth, TILE, axis, pieces[0].shape[1], 1.0)
    for piece in range(PIECES):
        rhs = place(rhs, 3 * PIECES + piece, -pieces[piece][axis:axis + 1])
    return rhs.astype(jnp.bfloat16)


def split(array):
    pieces = []
    rest = array
    for _ in range(PIECES):
        piece = rest.astype(jnp.bfloat16).astype(jnp.float32)
        pieces.append(piece)
        rest = rest - piece
    return pieces


def coefficients(rate_ref, bases, sigma):
    rate = [rate_ref[k] for k in range(bases)]
    decay = [-LOG2E * r for r in rate]
    slope = [(-2.0 * sigma) * r for r in rate]
    bend = [(4.0 * sigma) * r * r for r in rate]
    return decay, slope, bend


def pair_terms(delta, dots, coefs, sigma):
    decay, slope_coef, bend_coef = coefs
    bases = len(dots)
    square = delta[0] * delta[0] + delta[1] * delta[1] + delta[2] * delta[2]
    w = [jnp.exp2(decay[k] * square) * dots[k] for k in range(bases)]
    lh = (0.5 * sigma) * sum(w[1:], w[0])
    slope = sum([slope_coef[k] * w[k] for k in range(1, bases)], slope_coef[0] * w[0])
    bend = sum([bend_coef[k] * w[k] for k in range(1, bases)], bend_coef[0] * w[0])
    h = jnp.tanh(lh)
    u = 1.0 - h * h
    p1 = (1.0 + h) + lh * u
    p2 = u * (1.0 - lh * h)
    return p1 * slope, p2 * (slope * slope) + p1 * bend


def slot_terms(right, left, cols, separators, coefs, sigma, total, store):
    channels = left.shape[1] // len(coefs[0])
    rows = left.shape[0]
    parts = [jnp.dot(cols, r, preferred_element_type=jnp.float32) for r in separators]
    dots = [
        lax.dot_general(
            right[:, k * channels:(k + 1) * channels],
            left[:, k * channels:(k + 1) * channels],
            (((1,), (1,)), ((), ())),
            preferred_element_type=jnp.float32,
        )
        for k in range(len(coefs[0]))
    ]
    for start in range(0, rows, CHUNK):
        delta = [p[start:start + CHUNK] for p in parts]
        first, second = pair_terms(delta, [d[start:start + CHUNK] for d in dots], coefs, sigma)
        store(start, first, second)
        for a in range(3):
            total[a] = total[a] + jnp.sum((first * delta[a]).reshape(CHUNK // 8, 8, rows), axis=0)


def gather_rows(total, factor):
    return jnp.concatenate([factor * jnp.sum(t, axis=0, keepdims=True) for t in total], axis=0)


def project(x, embed_ref, wproj_ref):
    h = jnp.dot(x, embed_ref[...], preferred_element_type=jnp.float32)
    half_h = 0.5 * h
    hidden = (half_h + half_h * jnp.tanh(half_h)).astype(jnp.bfloat16)
    out = jnp.dot(hidden, wproj_ref[...], preferred_element_type=jnp.float32)
    return out.astype(jnp.bfloat16)


def own_kernel(slots, rate_ref, own_ref, pos_ref, embed_ref, wproj_ref,
               force_ref, first_ref, second_ref, tile_ref, proj_ref, sep_ref):
    rows, channels = own_ref.shape[1:]
    bases = wproj_ref.shape[1] // channels
    escale = 1.0 / math.sqrt(slots * rows)
    sigma = 1.0 / math.sqrt(channels)
    coefs = coefficients(rate_ref, bases, sigma)
    flat = own_ref[...].reshape(STEP_BLOCKS * rows, channels)
    proj_ref[...] = project(flat, embed_ref, wproj_ref).reshape(STEP_BLOCKS, rows, bases * channels)
    for part in range(STEP_BLOCKS):
        ones = jnp.ones((PIECES, rows), jnp.float32)
        zeros = jnp.zeros((TILE - 4 * PIECES, rows), jnp.float32)
        tile = jnp.concatenate(split(pos_ref[part]) + [ones, zeros], axis=0)
        tile_ref[part] = tile.astype(jnp.bfloat16)
        cols = jnp.transpose(tile).astype(jnp.bfloat16)
        separators = [difference_rhs(tile, a, TILE) for a in range(3)]
        for a in range(3):
            sep_ref[part, a] = separators[a]
        total = [jnp.zeros((8, rows), jnp.float32) for _ in range(3)]

        def store(start, first, second, part=part):
            first_ref[part, start:start + CHUNK, :] = first
            second_ref[part, start:start + CHUNK, :] = second

        left = proj_ref[part]
        slot_terms(left, left, cols, separators, coefs, sigma, total, store)
        force_ref[part] = gather_rows(total, -0.5 * escale)


def pair_kernel(
    nbr_ref, cnt_ref, rate_ref, meta_ref,
    own_proj, lo_a, lo_b, hi_a, hi_b, embed_ref, wproj_ref, own_tile, part_ref, sep_ref,
    force_ref, first_ref, second_ref, rows_ref,
    proj_ref, col_ref, sem,
):
    owned = own_tile.shape[0]
    half = lo_a.shape[0]
    slots = nbr_ref.shape[1]
    rows = first_ref.shape[2]
    channels = embed_ref.shape[0]
    bases = wproj_ref.shape[1] // channels
    escale = 1.0 / math.sqrt(slots * rows)
    sigma = 1.0 / math.sqrt(channels)
    step = pl.program_id(0)

    @pl.when(step == 0)
    def _():
        copy = pltpu.make_async_copy(own_proj, proj_ref.at[pl.ds(owned, owned)], sem)
        copy.start()

        def keep(tile, at):
            rows_ref[at] = tile
            col_ref[at] = jnp.transpose(tile.astype(jnp.float32)).astype(jnp.bfloat16)

        def take(source, base):
            def one(i, carry):
                x = source[pl.ds(2 * i, 2), pl.ds(0, rows), :].reshape(2 * rows, channels)
                out = project(x, embed_ref, wproj_ref)
                proj_ref[pl.ds(base + 2 * i, 2)] = out.reshape(2, rows, bases * channels)
                for j in range(2):
                    keep(source[2 * i + j, pl.ds(rows, TILE), :], base + 2 * i + j)
                return carry

            lax.fori_loop(0, half // 2, one, 0, unroll=4)

        near = meta_ref[1] * half
        far = half - near
        take(lo_a, near)
        take(hi_a, 2 * owned + near)
        take(lo_b, far)
        take(hi_b, 2 * owned + far)

        def own(i, carry):
            keep(own_tile[i], owned + i)
            return carry

        lax.fori_loop(0, owned, own, 0, unroll=4)
        copy.wait()

    coefs = coefficients(rate_ref, bases, sigma)
    offset = meta_ref[0]
    total_blocks = meta_ref[2]

    def one_block(part, carry):
        block = step * PAIR_BLOCKS + part
        count = cnt_ref[block]

        def run(live):
            left = proj_ref[owned + block]
            separators = [sep_ref[part, a] for a in range(3)]
            total = [jnp.zeros((8, rows), jnp.float32) for _ in range(3)]
            for slot in range(1, live):
                source = nbr_ref[block, slot] - offset
                source = jnp.where(source < 0, source + total_blocks, source)
                source = jnp.where(source >= total_blocks, source - total_blocks, source)

                def store(start, first, second, slot=slot):
                    first_ref[part, slot - 1, start:start + CHUNK, :] = first
                    second_ref[part, slot - 1, start:start + CHUNK, :] = second

                slot_terms(proj_ref[source], left, col_ref[source], separators, coefs, sigma, total, store)
            force_ref[part] = part_ref[part] + gather_rows(total, -0.5 * escale)

        for live in range(3, slots + 1):
            pl.when(count == live)(lambda live=live: run(live))
        return carry

    lax.fori_loop(0, PAIR_BLOCKS, one_block, 0)


def grad_slot(cols, sides, first_of, second_of, total):
    rows = cols.shape[0]
    parts = [jnp.dot(cols, r, preferred_element_type=jnp.float32) for r in sides]
    for start in range(0, rows, CHUNK):
        span = slice(start, start + CHUNK)
        delta = [p[span] for p in parts[:3]]
        change = [p[span] for p in parts[3:]]
        first = first_of(span)
        along = second_of(span) * (delta[0] * change[0] + delta[1] * change[1] + delta[2] * change[2])
        for a in range(3):
            term = first * change[a] + along * delta[a]
            total[a] = total[a] + jnp.sum(term.reshape(CHUNK // 8, 8, rows), axis=0)


def tangent_columns(tile, pieces):
    filler = jnp.zeros((TILE - 3 * PIECES, tile.shape[1]), jnp.float32)
    return jnp.transpose(jnp.concatenate([tile] + pieces + [filler], axis=0)).astype(jnp.bfloat16)


def own_grad_kernel(slots, tile_ref, tan_ref, first_ref, second_ref, grad_ref, side_ref):
    rows = first_ref.shape[1]
    escale = 1.0 / math.sqrt(slots * rows)
    for part in range(STEP_BLOCKS):
        tile = tile_ref[part].astype(jnp.float32)
        pieces = split(tan_ref[part])
        sides = [difference_rhs(tile, a, 2 * TILE) for a in range(3)]
        sides += [change_rhs(pieces, a, 2 * TILE) for a in range(3)]
        for n in range(6):
            side_ref[part, n] = sides[n]
        total = [jnp.zeros((8, rows), jnp.float32) for _ in range(3)]
        grad_slot(
            tangent_columns(tile, pieces), sides,
            lambda span, part=part: first_ref[part, span, :],
            lambda span, part=part: second_ref[part, span, :],
            total,
        )
        grad_ref[part] = gather_rows(total, 0.5 * escale)


def grad_kernel(
    nbr_ref, cnt_ref, meta_ref, pos_ref, tan_own, tan_lo, tan_hi,
    part_ref, side_ref, first_ref, second_ref,
    grad_ref, col_ref,
):
    owned = tan_own.shape[0]
    slots = nbr_ref.shape[1]
    rows = first_ref.shape[2]
    escale = 1.0 / math.sqrt(slots * rows)
    step = pl.program_id(0)

    @pl.when(step == 0)
    def _():
        def spread(tan, base):
            def one(i, carry):
                col_ref[base + i] = tangent_columns(pos_ref[base + i].astype(jnp.float32), split(tan[i]))
                return carry

            lax.fori_loop(0, owned, one, 0, unroll=4)

        spread(tan_lo, 0)
        spread(tan_own, owned)
        spread(tan_hi, 2 * owned)

    offset = meta_ref[0]
    total_blocks = meta_ref[2]

    def one_block(part, carry):
        block = step * PAIR_BLOCKS + part
        count = cnt_ref[block]

        def run(live):
            sides = [side_ref[part, n] for n in range(6)]
            total = [jnp.zeros((8, rows), jnp.float32) for _ in range(3)]
            for slot in range(1, live):
                source = nbr_ref[block, slot] - offset
                source = jnp.where(source < 0, source + total_blocks, source)
                source = jnp.where(source >= total_blocks, source - total_blocks, source)
                grad_slot(
                    col_ref[source], sides,
                    lambda span, slot=slot: first_ref[part, slot - 1, span, :],
                    lambda span, slot=slot: second_ref[part, slot - 1, span, :],
                    total,
                )
            grad_ref[part] = part_ref[part] + gather_rows(total, 0.5 * escale)

        for live in range(3, slots + 1):
            pl.when(count == live)(lambda live=live: run(live))
        return carry

    lax.fori_loop(0, PAIR_BLOCKS, one_block, 0)


def pack_kernel(meta_ref, feat_ref, pos_ref, out_ref):
    blocks, rows, _ = feat_ref.shape
    out_ref[:, pl.ds(0, rows), :] = feat_ref[...]
    ones = jnp.ones((PIECES, rows), jnp.float32)
    zeros = jnp.zeros((TILE - 4 * PIECES, rows), jnp.float32)
    for i in range(blocks):
        tile = jnp.concatenate(split(pos_ref[i]) + [ones, zeros], axis=0)
        out_ref[i, pl.ds(rows, TILE), :] = tile.astype(jnp.bfloat16)


def in_hbm(array):
    return pltpu.with_memory_space_constraint(array, pltpu.HBM)


def whole(array):
    return pl.BlockSpec(array.shape, lambda *_: (0,) * len(array.shape), pipeline_mode=pl.Buffered(1))


def stepped(shape, blocks=STEP_BLOCKS):
    return pl.BlockSpec((blocks,) + shape, lambda i, *_: (i,) + (0,) * len(shape))


def member_sum(array):
    size = lax.axis_size("member")
    others = [lax.ppermute(array, "member", flip("member", bit)) for bit in range(1, size)]
    return array + others[0] + (others[1] + others[2])


def body(positions, features, nbr_list, nbr_count, w_embed, w_proj, rates):
    owned, dims, rows = positions.shape
    channels = features.shape[2]
    slots = nbr_list.shape[1]
    width = w_proj.shape[2]
    domains = lax.axis_size("space")
    members = lax.axis_size("member")
    domain = lax.axis_index("space")
    core = lax.axis_index("member") % 2
    up, down = ring("space", 1), ring("space", -1)
    half = owned // 2

    offset = (domain - 1) * owned
    meta = jnp.stack([offset, core, jnp.int32(domains * owned)]).astype(jnp.int32)
    embed, proj = in_hbm(w_embed[0]), in_hbm(w_proj[0])
    rate, counts = in_hbm(rates[0]), in_hbm(nbr_count)
    mine = pl.pallas_call(
        pack_kernel,
        grid_spec=pltpu.PrefetchScalarGridSpec(
            num_scalar_prefetch=1,
            grid=(1,),
            in_specs=[
                pl.BlockSpec((half, rows, channels), lambda i, m: (m[1], 0, 0)),
                pl.BlockSpec((half, dims, rows), lambda i, m: (m[1], 0, 0)),
            ],
            out_specs=pl.BlockSpec((half, rows + TILE, channels), lambda i, m: (0, 0, 0)),
        ),
        out_shape=jax.ShapeDtypeStruct((half, rows + TILE, channels), jnp.bfloat16),
        compiler_params=pltpu.CompilerParams(vmem_limit_bytes=8 << 20),
        name="pack_halo",
    )(meta, in_hbm(features), positions)
    lo_a = lax.ppermute(mine, "space", up)
    hi_a = lax.ppermute(mine, "space", down)
    pair = (rows, rows)
    selfs = jax.ShapeDtypeStruct((owned,) + pair, jnp.float32)
    pairs = jax.ShapeDtypeStruct((owned, slots - 1) + pair, jnp.float32)
    small = jax.ShapeDtypeStruct((owned, dims, rows), jnp.float32)
    tiles = jax.ShapeDtypeStruct((owned, TILE, rows), jnp.bfloat16)
    window = jax.ShapeDtypeStruct((3 * owned, TILE, rows), jnp.bfloat16)
    table = jax.ShapeDtypeStruct((owned, rows, width), jnp.bfloat16)
    separate = jax.ShapeDtypeStruct((owned, dims, TILE, rows), jnp.bfloat16)
    sides = jax.ShapeDtypeStruct((owned, 2 * dims, 2 * TILE, rows), jnp.bfloat16)
    steps = (owned // STEP_BLOCKS,)
    part_force, own_first, own_second, own_tile, own_proj, separators = pl.pallas_call(
        functools.partial(own_kernel, slots),
        grid_spec=pltpu.PrefetchScalarGridSpec(
            num_scalar_prefetch=1,
            grid=steps,
            in_specs=[stepped((rows, channels)), stepped((dims, rows)), whole(w_embed[0]), whole(w_proj[0])],
            out_specs=[
                stepped((dims, rows)), stepped(pair), stepped(pair),
                stepped((TILE, rows)), stepped((rows, width)), stepped((dims, TILE, rows)),
            ],
        ),
        out_shape=[small, selfs, selfs, tiles, table, separate],
        compiler_params=pltpu.CompilerParams(vmem_limit_bytes=8 << 20),
        name="own_pairs",
    )(rate, in_hbm(features), positions, embed, proj)
    lo_a, hi_a, own_tile = lax.optimization_barrier((lo_a, hi_a, own_tile))
    swap = flip("member", 1)
    lo_b = lax.ppermute(lo_a, "member", swap)
    hi_b = lax.ppermute(hi_a, "member", swap)
    halo = (lo_a, lo_b, hi_a, hi_b, embed, proj, own_tile)
    force, first, second, pos_rows = pl.pallas_call(
        pair_kernel,
        grid_spec=pltpu.PrefetchScalarGridSpec(
            num_scalar_prefetch=4,
            grid=(owned // PAIR_BLOCKS,),
            in_specs=[pl.BlockSpec(memory_space=pl.ANY)] + [whole(t) for t in halo] + [stepped((dims, rows), PAIR_BLOCKS), stepped((dims, TILE, rows), PAIR_BLOCKS)],
            out_specs=[
                stepped((dims, rows), PAIR_BLOCKS), stepped((slots - 1,) + pair, PAIR_BLOCKS), stepped((slots - 1,) + pair, PAIR_BLOCKS), whole(window),
            ],
            scratch_shapes=[
                pltpu.VMEM((3 * owned, rows, width), jnp.bfloat16),
                pltpu.VMEM((3 * owned, rows, TILE), jnp.bfloat16),
                pltpu.SemaphoreType.DMA,
            ],
        ),
        out_shape=[small, pairs, pairs, window],
        compiler_params=pltpu.CompilerParams(vmem_limit_bytes=18 << 20),
        name="halo_pairs",
    )(nbr_list, counts, rate, meta, own_proj, *halo, in_hbm(part_force), separators)

    mean_force = member_sum(force) / members
    tangent = (2.0 / members) * (force - mean_force)
    tan_lo = lax.ppermute(tangent, "space", up)
    tan_hi = lax.ppermute(tangent, "space", down)
    part_grad, side_table = pl.pallas_call(
        functools.partial(own_grad_kernel, slots),
        grid=steps,
        in_specs=[stepped((TILE, rows)), stepped((dims, rows)), stepped(pair), stepped(pair)],
        out_specs=[stepped((dims, rows)), stepped((2 * dims, 2 * TILE, rows))],
        out_shape=[small, sides],
        compiler_params=pltpu.CompilerParams(vmem_limit_bytes=8 << 20),
        name="own_gradient",
    )(own_tile, tangent, in_hbm(own_first), in_hbm(own_second))
    tensors = (pos_rows, tangent, tan_lo, tan_hi)
    grad = pl.pallas_call(
        grad_kernel,
        grid_spec=pltpu.PrefetchScalarGridSpec(
            num_scalar_prefetch=3,
            grid=(owned // PAIR_BLOCKS,),
            in_specs=[whole(t) for t in tensors] + [stepped((dims, rows), PAIR_BLOCKS), stepped((2 * dims, 2 * TILE, rows), PAIR_BLOCKS)] + [stepped((slots - 1,) + pair, PAIR_BLOCKS)] * 2,
            out_specs=stepped((dims, rows), PAIR_BLOCKS),
            scratch_shapes=[pltpu.VMEM((3 * owned, rows, 2 * TILE), jnp.bfloat16)],
        ),
        out_shape=small,
        compiler_params=pltpu.CompilerParams(vmem_limit_bytes=10 << 20),
        name="variance_gradient",
    )(nbr_list, counts, meta, *tensors, part_grad, side_table, first, second)
    return (mean_force, member_sum(grad))


def solution(mesh):
    return jax.shard_map(
        body,
        mesh=mesh,
        in_specs=(
            P("space", None, None),
            P("space", None, None),
            P("space", None),
            P("space"),
            P("member", None, None),
            P("member", None, None),
            P("member", None),
        ),
        out_specs=(P("space", None, None), P("space", None, None)),
        check_vma=False,
    )
```
